256 devices in a mesh: section: 2 (over core), seq: 32 (over x, z), chan: 4 (over y).
Axes of the slice: x: 4, y: 4, z: 8, core: 2. Of those that a mesh axis runs over, the one named last changes fastest.
Arguments:
- layer_inputs: bfloat16 [2, 4, 2048, 4096], P('section', None, 'seq', 'chan')
- out_grad: bfloat16 [4, 2048, 4096], P(None, 'seq', 'chan')
- rate_weight: bfloat16 [2, 16, 256, 256], P('section', 'chan'), may hold values from -0.375 to 0.375
- input_weight: bfloat16 [2, 16, 256, 256], P('section', 'chan'), may hold values from -0.375 to 0.375
- rate_bias: float32 [2, 4096], P('section', 'chan'), may hold values from -4 to 4
- input_bias: float32 [2, 4096], P('section', 'chan'), may hold values from -4 to 4
- decay_param: float32 [2, 4096], P('section', 'chan')
- norm_gain: float32 [2, 4096], P('section', 'chan'), may hold values from 0.1 to 1.9
- doc_starts: int32 [4, 3], replicated, may hold values from 1 to 2047
Outputs:
- input_grads: bfloat16 [2, 4, 2048, 4096], P('section', None, 'seq', 'chan')
- rate_weight_grad: float32 [2, 16, 256, 256], P('section', 'chan')
- input_weight_grad: float32 [2, 16, 256, 256], P('section', 'chan')
- vector_grads: float32 [2, 3, 4096], P('section', None, 'chan')
The draws below stay inside these ranges and needn't reach their ends.
All inputs are finite; a program needn't handle non-finite values.
Results may differ from the reference program's by a relative error of at most 0.0055.
Values may be sent and summed in bfloat16 or wider, within the bound.
A program may use at most 64 MiB of HBM per device.

```python
import math
import jax
import jax.numpy as jnp
from jax import lax

D = 4096
HEADS = 16
HEAD = 256
MICRO = 4
DOCS = 3
LAYERS = 2
SEQ_LEN = 2048


def draw_layer_inputs(key, part):
    key_base = jax.random.fold_in(key, 0)
    key_column = jax.random.fold_in(key, 1)
    key_row = jax.random.fold_in(key, 2)
    key_sign = jax.random.fold_in(key, 4)
    key_level = jax.random.fold_in(key, 5)
    full_shape = (LAYERS, MICRO, SEQ_LEN, D)
    column_pos = jnp.arange(D, dtype=jnp.float32) / D
    column_scale = jnp.exp(column_pos * math.log(3.0) + jax.random.uniform(key_column, (D,), jnp.float32, 0.0, math.log(3.3)))
    row_scale = jnp.exp(jax.random.uniform(key_row, (LAYERS, MICRO, SEQ_LEN, 1), jnp.float32, 0.0, math.log(4.0)))
    offset_sign = jnp.where(jax.random.uniform(key_sign, (LAYERS, MICRO, 1, D), jnp.float32) < 0.5, -1.0, 1.0)
    offset_level = jax.random.uniform(key_level, (LAYERS, MICRO, 1, D), jnp.float32, 0.3, 0.7)
    channel_offset = offset_sign * offset_level
    base_draw = jax.random.normal(key_base, full_shape, jnp.float32)
    return ((base_draw + channel_offset) * row_scale * column_scale).astype(jnp.bfloat16)


def draw_out_grad(key, part):
    key_base = jax.random.fold_in(key, 0)
    key_column = jax.random.fold_in(key, 1)
    key_sign = jax.random.fold_in(key, 3)
    key_level = jax.random.fold_in(key, 4)
    full_shape = (MICRO, SEQ_LEN, D)
    ramp_scale = jnp.exp(jnp.arange(SEQ_LEN, dtype=jnp.float32) / SEQ_LEN * math.log(3.0))[None, :, None]
    column_scale = jnp.exp(jax.random.uniform(key_column, (D,), jnp.float32, 0.0, math.log(3.0)))
    offset_sign = jnp.where(jax.random.uniform(key_sign, (MICRO, 1, D), jnp.float32) < 0.5, -1.0, 1.0)
    offset_level = jax.random.uniform(key_level, (MICRO, 1, D), jnp.float32, 0.03, 0.07)
    channel_offset = offset_sign * offset_level
    base_draw = jax.random.normal(key_base, full_shape, jnp.float32)
    return ((base_draw + channel_offset) * ramp_scale * column_scale).astype(jnp.bfloat16)


def draw_decay_param(key, part):
    key_mask, key_fast, key_slow = jax.random.split(key, 3)
    fast_share = 0.5
    fast_mask = jax.random.uniform(key_mask, (LAYERS, D), jnp.float32) < fast_share
    rate_fast = jnp.exp(jax.random.uniform(key_fast, (LAYERS, D), jnp.float32, math.log(0.004), math.log(0.02)))
    rate_slow = jnp.exp(jax.random.uniform(key_slow, (LAYERS, D), jnp.float32, math.log(0.02 / SEQ_LEN), math.log(0.25 / SEQ_LEN)))
    rate_value = jnp.where(fast_mask, rate_fast, rate_slow)
    return -jnp.log(jnp.expm1(rate_value))


def touch_ends(values, rng, low, top_value):
    shape = values.shape
    index_at = [jax.random.randint(jax.random.fold_in(rng, axis), (), 0, shape[axis]) for axis in range(len(shape))]
    values = values.at[tuple(index_at)].set(low)
    longest = shape.index(max(shape))
    index_at[longest] = (index_at[longest] + 1) % shape[longest]
    return values.at[tuple(index_at)].set(top_value)


def level_of(rng, shape, pieces, smallest, top_value):
    loudness = 1.0
    for dim, shards_of in pieces:
        heights = jax.random.uniform(jax.random.fold_in(jax.random.fold_in(rng, 6), dim), (shards_of,), jnp.float32, smallest / len(pieces), top_value / len(pieces))
        loudness = loudness * jnp.repeat(jnp.exp(heights), shape[dim] // shards_of).reshape((-1,) + (1,) * (len(shape) - 1 - dim))
    return loudness


def bell_draw(own_key, dims, spread, most, cuts=(), kind=jnp.bfloat16):
    entries = spread * jax.random.normal(own_key, dims, jnp.float32)
    if cuts:
        entries = entries * level_of(own_key, dims, cuts, -0.22, 0.18)
    return jnp.clip(entries, -most, most).astype(kind)


def setup_inputs(seed: int = 0) -> dict:
    key_of = jax.random.split(jax.random.key(seed), 10)
    return {
        "layer_inputs": draw_layer_inputs(jax.random.fold_in(key_of[9], 71), 0),
        "out_grad": draw_out_grad(jax.random.fold_in(key_of[9], 71), 0),
        "rate_weight": bell_draw(key_of[2], (LAYERS, HEADS, HEAD, HEAD), HEAD ** -0.5, 0.375, ((0, 2), (1, 4))),
        "input_weight": bell_draw(key_of[3], (LAYERS, HEADS, HEAD, HEAD), HEAD ** -0.5, 0.375, ((0, 2), (1, 4))),
        "rate_bias": bell_draw(key_of[4], (LAYERS, D), 1.0, 4.0, ((0, 2), (1, 4)), jnp.float32),
        "input_bias": bell_draw(key_of[5], (LAYERS, D), 1.0, 4.0, ((0, 2), (1, 4)), jnp.float32),
        "decay_param": draw_decay_param(jax.random.fold_in(key_of[9], 71), 0),
        "norm_gain": jnp.clip(1.0 + 0.18 * jax.random.normal(key_of[7], (LAYERS, D), jnp.float32), 0.1, 1.9),
        "doc_starts": touch_ends(jax.random.randint(key_of[8], (MICRO, DOCS), 1, SEQ_LEN), jax.random.fold_in(key_of[8], 1), 1, SEQ_LEN - 1).astype(jnp.int32),
    }


def pair_combine(first_pair, second_pair):
    return (first_pair[0] * second_pair[0], second_pair[0] * first_pair[1] + second_pair[1])

def layer_backward(inputs, upstream, weights_both, bias_both, decay_row, gain_row, starts):
    seq_rows = inputs.shape[0]
    xfloat = inputs.astype(jnp.float32)
    inv_rms = lax.rsqrt(lax.optimization_barrier(jnp.sum(xfloat * xfloat, axis=1, keepdims=True)) / D + 1e-06)
    normed = (xfloat * inv_rms * gain_row).astype(jnp.bfloat16)
    normed_wide = normed.astype(jnp.float32)
    by_head = normed_wide.reshape(seq_rows, HEADS, HEAD)
    pre_both = jnp.einsum('shb,hbc->shc', by_head, weights_both.astype(jnp.float32))
    pre_rate = pre_both[:, :, :HEAD].reshape(seq_rows, D) + bias_both[0]
    pre_input = pre_both[:, :, HEAD:].reshape(seq_rows, D) + bias_both[1]
    rate_gate = jax.nn.sigmoid(pre_rate)
    input_gate = jax.nn.sigmoid(pre_input)
    soft_rate = jax.nn.softplus(-decay_row)
    log_decay = -8.0 * rate_gate * soft_rate
    position = jnp.arange(seq_rows, dtype=jnp.int32)
    is_reset = jnp.logical_or(position == 0, jnp.any(position[:, None] == starts[None, :], axis=1))[:, None]
    decay_eff = jnp.where(is_reset, 0.0, jnp.exp(log_decay))
    square_gap = jnp.exp(2.0 * log_decay)
    base_mult = jnp.sqrt(jnp.maximum(-jnp.expm1(2.0 * log_decay), 1e-06))
    multiplier = jnp.where(is_reset, 1.0, base_mult)
    lru_drive = multiplier * input_gate * normed_wide
    decay_prod, states = lax.associative_scan(pair_combine, (decay_eff, lru_drive), axis=0)
    prev_state = jnp.concatenate([jnp.zeros((1, D), jnp.float32), states[:-1]], axis=0)
    upstream_wide = upstream.astype(jnp.float32)
    next_decay = jnp.concatenate([decay_eff[1:], jnp.ones((1, D), jnp.float32)], axis=0)
    flip_pair = lax.associative_scan(pair_combine, (next_decay[::-1], upstream_wide[::-1]), axis=0)
    state_grad = flip_pair[1][::-1]
    grad_mult = state_grad * input_gate * normed_wide
    grad_log = state_grad * prev_state * decay_eff - jnp.where(is_reset, 0.0, grad_mult * square_gap / base_mult)
    grad_rate = (grad_log * (-8.0 * soft_rate) * rate_gate * (1.0 - rate_gate)).astype(jnp.bfloat16)
    grad_input = (state_grad * multiplier * normed_wide * input_gate * (1.0 - input_gate)).astype(jnp.bfloat16)
    grad_both = jnp.concatenate([grad_rate.reshape(seq_rows, HEADS, HEAD), grad_input.reshape(seq_rows, HEADS, HEAD)], axis=2).astype(jnp.float32)
    back_proj = jnp.einsum('shc,hbc->shb', grad_both, weights_both.astype(jnp.float32)).reshape(seq_rows, D)
    grad_normed = state_grad * multiplier * input_gate + back_proj
    scaled = grad_normed * gain_row
    cross_sum = lax.optimization_barrier(jnp.sum(xfloat * scaled, axis=1, keepdims=True)) / D
    input_grad = (upstream_wide + inv_rms * scaled - xfloat * inv_rms ** 3 * cross_sum).astype(jnp.bfloat16)
    weight_term = jnp.einsum('shb,shc->hbc', by_head, grad_both)
    vector_term = jnp.stack([lax.optimization_barrier(jnp.sum(grad_rate.astype(jnp.float32), axis=0)), lax.optimization_barrier(jnp.sum(grad_input.astype(jnp.float32), axis=0)), lax.optimization_barrier(jnp.sum(grad_normed * xfloat * inv_rms, axis=0))])
    return (input_grad, weight_term, vector_term)

def reference(layer_inputs, out_grad, rate_weight, input_weight, rate_bias, input_bias, decay_param, norm_gain, doc_starts):
    grad_scale = 1.0 / math.sqrt(MICRO * SEQ_LEN)
    upstream_list = [out_grad[micro_index] for micro_index in range(MICRO)]
    layer_grads = [None] * LAYERS
    layer_weights = [None] * LAYERS
    layer_vectors = [None] * LAYERS
    for layer_index in range(LAYERS - 1, -1, -1):
        weights_both = jnp.concatenate([rate_weight[layer_index], input_weight[layer_index]], axis=2)
        bias_both = jnp.stack([rate_bias[layer_index], input_bias[layer_index]])
        weight_total = jnp.zeros((HEADS, HEAD, 2 * HEAD), jnp.float32)
        vector_total = jnp.zeros((3, D), jnp.float32)
        results = []
        for micro_index in range(MICRO):
            input_grad, weight_term, vector_term = layer_backward(layer_inputs[layer_index, micro_index], upstream_list[micro_index], weights_both, bias_both, decay_param[layer_index], norm_gain[layer_index], doc_starts[micro_index])
            results.append(input_grad)
            weight_total = weight_total + weight_term
            vector_total = vector_total + vector_term
        upstream_list = results
        layer_grads[layer_index] = jnp.stack(results)
        layer_weights[layer_index] = weight_total * grad_scale
        layer_vectors[layer_index] = vector_total * grad_scale
    weight_stack = jnp.stack(layer_weights)
    return (jnp.stack(layer_grads), weight_stack[:, :, :, :HEAD], weight_stack[:, :, :, HEAD:], jnp.stack(layer_vectors))
```

```python
import math

import jax
import jax.numpy as jnp
from jax import lax
from jax.experimental import pallas as pl
from jax.experimental.pallas import tpu as pltpu
from jax.sharding import PartitionSpec as P

F32 = jnp.float32
BF16 = jnp.bfloat16
NX, NZ, NY = 4, 8, 4
MICRO, ROWS, WIDTH = 4, 64, 1024
HEADS, HEAD = 4, 256
FULL = WIDTH * NY
GROUPS = 2
MG = MICRO // GROUPS
GR = MG * ROWS
MESH = pl.DeviceIdType.MESH


def dot(a, b):
    return jnp.dot(a, b, preferred_element_type=F32)


def dot_t(a, b):
    return lax.dot_general(a, b, (((1,), (1,)), ((), ())), preferred_element_type=F32)


def sublane(shape):
    return lax.broadcasted_iota(jnp.int32, shape, 0)


def lane(shape):
    return lax.broadcasted_iota(jnp.int32, shape, 1)


def log1p_of(v):
    series = v * (1.0 - v * (0.5 - v * (1.0 / 3.0 - v * (0.25 - v * 0.2))))
    return jnp.where(v < 0.03125, series, jnp.log(1.0 + v))


def body(
    x_hbm, up_hbm, rw_hbm, iw_hbm, rb_ref, ib_ref, dp_ref, gain_ref, starts_ref,
    ig_hbm, wg_hbm, vec_ref,
    xv, upv, rwv, iwv, xp, nd, dec, drv, mi, rr, kk, cc, upp, sv, dg, gb, keep, invb, inv_t, fb,
    ea, eh, eba, ebq, pa_s, fzs, fzr, fxs, fxr, bzs, bzr, bxs, bxr, stin, qin, zpre, zsuf,
    s1, s1r, ca, s2, s2r, igv, vacc, vzs, vzr, vxs, vxr,
    ndt, wgb, rx, rs1, rz, wgo,
    loc_sem, out_sem, wout_sem, s1_ss, s1_rs, s2_ss, s2_rs, fz_ss, fz_rs, fx_ss, fx_rs, bz_ss, bz_rs, bx_ss, bx_rs,
    up_ss, up_rs, vz_ss, vz_rs, vx_ss, vx_rs, rx_ss, rx_rs, rz_ss, rz_rs, az_ss, az_rs, ax_ss, ax_rs,
):
    sec = lax.axis_index("section")
    seq = lax.axis_index("seq")
    chan = lax.axis_index("chan")
    x_at = seq // NZ
    z_at = seq % NZ

    def z_peer(d):
        return {"seq": x_at * NZ + (z_at + d) % NZ}

    def x_peer(d):
        return {"seq": ((x_at + d) % NX) * NZ + z_at}

    def y_peer(d):
        return {"chan": (chan + d) % NY}

    other_core = {"section": 1 - sec}

    def remote(src, dst, ss, rs, to):
        return pltpu.make_async_remote_copy(
            src_ref=src, dst_ref=dst, send_sem=ss, recv_sem=rs, device_id=to, device_id_type=MESH
        )

    loads = [pltpu.make_async_copy(x_hbm.at[0], xv, loc_sem.at[0])]
    w_loads = [
        pltpu.make_async_copy(rw_hbm.at[0], rwv, loc_sem.at[1]),
        pltpu.make_async_copy(iw_hbm.at[0], iwv, loc_sem.at[2]),
    ]
    up_load = pltpu.make_async_copy(up_hbm, upv, loc_sem.at[3])
    for c in loads + w_loads:
        c.start()

    @pl.when(sec == 1)
    def _():
        up_load.start()

    barrier = pltpu.get_barrier_semaphore()
    peers = [z_peer(d) for d in range(1, NZ)] + [x_peer(d) for d in range(1, NX)]
    peers += [y_peer(d) for d in range(1, NY)] + [other_core]
    for to in peers:
        pl.semaphore_signal(barrier, inc=1, device_id=to, device_id_type=MESH)

    r_i = sublane((ROWS, ROWS))
    t_i = lane((ROWS, ROWS))
    perm = jnp.where(t_i == (r_i % 8) * 8 + r_i // 8, 1.0, 0.0).astype(BF16)
    perm_back = jnp.where(r_i == (t_i % 8) * 8 + t_i // 8, 1.0, 0.0).astype(BF16)

    r_w = sublane((ROWS, HEAD))
    position = seq * ROWS + (r_w % 8) * 8 + r_w // 8
    for m in range(MICRO):
        reset = position == 0
        for d in range(3):
            reset = jnp.logical_or(reset, position == starts_ref[m, d])
        keep[m] = jnp.where(reset, 0.0, 1.0)
    vacc[...] = jnp.zeros_like(vacc)
    ca[...] = jnp.zeros_like(ca)


    for c in loads:
        c.wait()
    lane_t = lane((8, 128))
    tile = jnp.zeros((8, 128), F32)
    for m in range(MICRO):
        x_m = dot(perm, xv[m])
        acc = jnp.zeros((ROWS, 128), F32)
        for k in range(HEADS):
            x_k = x_m[:, k * HEAD : (k + 1) * HEAD]
            xp[k, m * ROWS : (m + 1) * ROWS, :] = x_k
            sq = x_k * x_k
            acc = acc + (sq[:, :128] + sq[:, 128:])
        for j in range(8):
            col = jnp.sum(acc[j * 8 : j * 8 + 8], axis=1, keepdims=True)
            tile = jnp.where(lane_t == m * 8 + j, col, tile)
    s1[...] = tile
    pl.semaphore_wait(barrier, len(peers))
    s1_copies = [
        remote(s1, s1r.at[d - 1], s1_ss.at[d - 1], s1_rs.at[d - 1], y_peer(d)) for d in range(1, NY)
    ]
    for c in s1_copies:
        c.start()
    for c in w_loads:
        c.wait()
    for c in s1_copies:
        c.wait_recv()
    inv_tile = lax.rsqrt((s1[...] + s1r[0] + s1r[1] + s1r[2]) / FULL + 1e-06)
    inv_t[...] = inv_tile
    for m in range(MICRO):
        for j in range(8):
            at = m * 8 + j
            invb[m, j * 8 : j * 8 + 8, :] = jnp.broadcast_to(inv_tile[:, at : at + 1], (8, HEAD))

    sub = sublane((8, HEAD))

    def scan_up(a, h):
        for sh in (1, 2, 4):
            ok = sub >= sh
            h = h + a * jnp.where(ok, pltpu.roll(h, sh, 0), 0.0)
            a = a * jnp.where(ok, pltpu.roll(a, sh, 0), 1.0)
        return a, h

    def scan_down(a, h):
        for sh in (1, 2, 4):
            ok = sub < 8 - sh
            h = h + a * jnp.where(ok, pltpu.roll(h, 8 - sh, 0), 0.0)
            a = a * jnp.where(ok, pltpu.roll(a, 8 - sh, 0), 1.0)
        return a, h

    def to_tile(ref, index, k, row):
        for half in range(2):
            ref[(*index, pl.ds(k * 2 + half, 1), slice(None))] = row[:, half * 128 : half * 128 + 128]

    def from_tile(ref, index, k):
        return jnp.concatenate(
            [ref[(*index, pl.ds(k * 2 + half, 1), slice(None))] for half in range(2)], axis=1
        )

    def head_lanes(k):
        return pl.ds(pl.multiple_of(k * HEAD, HEAD), HEAD)

    def forward_head(g, k):
        gain = gain_ref[:, head_lanes(k)]
        rb = rb_ref[:, head_lanes(k)]
        ib = ib_ref[:, head_lanes(k)]
        v = dp_ref[:, head_lanes(k)]
        rate = -8.0 * (jnp.maximum(-v, 0.0) + log1p_of(jnp.exp(-jnp.abs(v))))
        for m in range(g * MG, (g + 1) * MG):
            rows = slice(m * ROWS, (m + 1) * ROWS)
            nd[k, rows, :] = (xp[k, rows, :] * invb[m] * gain).astype(BF16)
        grow = slice(g * GR, (g + 1) * GR)
        n_g = nd[k, grow, :]
        pre_r = dot(n_g, rwv[k])
        pre_i = dot(n_g, iwv[k])
        for m in range(g * MG, (g + 1) * MG):
            rows = slice(m * ROWS, (m + 1) * ROWS)
            own = slice((m - g * MG) * ROWS, (m - g * MG + 1) * ROWS)
            rg = 0.5 * jnp.tanh(0.5 * (pre_r[own] + rb)) + 0.5
            ig = 0.5 * jnp.tanh(0.5 * (pre_i[own] + ib)) + 0.5
            nw = n_g[own].astype(F32)
            kept = keep[m]
            ld = rate * rg
            e = jnp.exp(ld)
            gap = e * e
            u = ld + ld
            series = -u * (1.0 + u * (0.5 + u * (1.0 / 6.0 + u * (1.0 / 24.0 + u * (1.0 / 120.0)))))
            em = jnp.where(u > -0.125, series, 1.0 - gap)
            em = jnp.maximum(em, 1e-06)
            rs = lax.rsqrt(em)
            mult = jnp.where(kept > 0.5, em * rs, 1.0)
            a = e * kept
            mig = mult * ig
            b = mig * nw
            dec[k, rows, :] = a
            drv[k, rows, :] = b
            mi[k, rows, :] = mig
            rr[k, rows, :] = kept * (ig * nw * gap * rs)
            kk[k, rows, :] = ld * (1.0 - rg)
            cc[k, rows, :] = b * (1.0 - ig)
            pa = a[:8]
            h = b[:8]
            for j in range(1, 8):
                a_j = a[j * 8 : j * 8 + 8]
                h = a_j * h + b[j * 8 : j * 8 + 8]
                pa = pa * a_j
            seg = slice(m * 8, m * 8 + 8)
            pa_s[k, seg, :] = pa
            a_in, h_in = scan_up(pa, h)
            ea[k, seg, :] = jnp.where(sub >= 1, pltpu.roll(a_in, 1, 0), 1.0)
            eh[k, seg, :] = jnp.where(sub >= 1, pltpu.roll(h_in, 1, 0), 0.0)
            to_tile(fzs, (m, 0), k, a_in[7:8])
            to_tile(fzs, (m, 1), k, h_in[7:8])

    def group(g):
        return pl.ds(g * MG, MG)

    def fz(g, d):
        return remote(
            fzs.at[group(g)], fzr.at[d - 1, group(g)], fz_ss.at[g, d - 1], fz_rs.at[g, d - 1], z_peer(d)
        )

    def fx(g, d):
        return remote(
            fxs.at[group(g)], fxr.at[d - 1, group(g)], fx_ss.at[g, d - 1], fx_rs.at[g, d - 1], x_peer(d)
        )

    def bz(g, d):
        return remote(
            bzs.at[group(g)], bzr.at[d - 1, group(g)], bz_ss.at[g, d - 1], bz_rs.at[g, d - 1], z_peer(d)
        )

    def bx(g, d):
        return remote(
            bxs.at[group(g)], bxr.at[d - 1, group(g)], bx_ss.at[g, d - 1], bx_rs.at[g, d - 1], x_peer(d)
        )

    for g in range(GROUPS):

        def fwd_k(k, carry, g=g):
            forward_head(g, k)
            return carry

        lax.fori_loop(0, HEADS, fwd_k, 0)
        for d in range(1, NZ):
            fz(g, d).start()

    def back_local(g):
        for m in range(g * MG, (g + 1) * MG):
            u_m = dot(perm, upv[m])
            for k in range(HEADS):
                upp[k, m * ROWS : (m + 1) * ROWS, :] = u_m[:, k * HEAD : (k + 1) * HEAD]

        def local_k(k, carry):
            for m in range(g * MG, (g + 1) * MG):
                q = jnp.zeros((8, HEAD), F32)
                for j in range(7, -1, -1):
                    at = slice(m * ROWS + j * 8, m * ROWS + j * 8 + 8)
                    q = dec[k, at, :] * (upp[k, at, :] + q)
                seg = slice(m * 8, m * 8 + 8)
                a_in, q_in = scan_down(pa_s[k, seg, :], q)
                eba[k, seg, :] = jnp.where(sub < 7, pltpu.roll(a_in, 7, 0), 1.0)
                ebq[k, seg, :] = jnp.where(sub < 7, pltpu.roll(q_in, 7, 0), 0.0)
                to_tile(bzs, (m,), k, q_in[0:1])
            return carry

        lax.fori_loop(0, HEADS, local_k, 0)
        for d in range(1, NZ):
            bz(g, d).start()

    @pl.when(sec == 1)
    def _():
        up_load.wait()
        for g in range(GROUPS):
            back_local(g)

    def turn_k(k, carry):
        ndt[k] = nd[k].T
        return carry

    lax.fori_loop(0, HEADS, turn_k, 0)

    for g in range(GROUPS):
        for d in range(1, NZ):
            fz(g, d).wait_recv()
        for m in range(g * MG, (g + 1) * MG):
            a_own, h_own = fzs[m, 0], fzs[m, 1]
            a_pre, h_pre = jnp.ones((8, 128), F32), jnp.zeros((8, 128), F32)
            a_suf, h_suf = a_pre, h_pre
            for d in range(1, NZ):
                ok = z_at >= d
                h_pre = h_pre + a_pre * jnp.where(ok, fzr[d - 1, m, 1], 0.0)
                a_pre = a_pre * jnp.where(ok, fzr[d - 1, m, 0], 1.0)
                ok = z_at + d < NZ
                a_d = jnp.where(ok, fzr[NZ - d - 1, m, 0], 1.0)
                h_suf = jnp.where(ok, fzr[NZ - d - 1, m, 1], 0.0) + a_d * h_suf
                a_suf = a_suf * a_d
            zpre[m, 0] = a_pre
            zpre[m, 1] = h_pre
            zsuf[m] = a_suf
            fxs[m, 0] = a_pre * a_own * a_suf
            fxs[m, 1] = h_suf + a_suf * (h_own + a_own * h_pre)
        for d in range(1, NX):
            fx(g, d).start()

    def up_copy(g):
        return remote(igv.at[group(g)], upv.at[group(g)], up_ss.at[g], up_rs.at[g], other_core)

    @pl.when(sec == 0)
    def _():
        for g in range(GROUPS):
            up_copy(g).wait_recv()
            back_local(g)

    for g in range(GROUPS):
        for d in range(1, NZ):
            bz(g, d).wait_recv()
        for m in range(g * MG, (g + 1) * MG):
            a_run, q_run = jnp.ones((8, 128), F32), jnp.zeros((8, 128), F32)
            for d in range(1, NZ):
                ok = z_at + d < NZ
                q_run = q_run + a_run * jnp.where(ok, bzr[NZ - d - 1, m], 0.0)
                a_run = a_run * jnp.where(ok, fzr[NZ - d - 1, m, 0], 1.0)
            qin[m] = q_run
            total = bzs[m] + fzs[m, 0] * q_run
            for d in range(1, NZ):
                ok = z_at >= d
                total = jnp.where(ok, bzr[d - 1, m] + fzr[d - 1, m, 0] * total, total)
            bxs[m] = total
        for d in range(1, NX):
            bx(g, d).start()

    for g in range(GROUPS):
        for d in range(1, NX):
            fx(g, d).wait_recv()
        for m in range(g * MG, (g + 1) * MG):
            a_run, h_run = jnp.ones((8, 128), F32), jnp.zeros((8, 128), F32)
            for d in range(1, NX):
                ok = x_at >= d
                h_run = h_run + a_run * jnp.where(ok, fxr[d - 1, m, 1], 0.0)
                a_run = a_run * jnp.where(ok, fxr[d - 1, m, 0], 1.0)
            stin[m] = zpre[m, 1] + zpre[m, 0] * h_run

    def s2_copy(g, d):
        return remote(s2.at[g], s2r.at[g, d - 1], s2_ss.at[g, d - 1], s2_rs.at[g, d - 1], y_peer(d))

    for g in range(GROUPS):
        for d in range(1, NX):
            bx(g, d).wait_recv()
        for m in range(g * MG, (g + 1) * MG):
            a_run, q_run = jnp.ones((8, 128), F32), jnp.zeros((8, 128), F32)
            for d in range(1, NX):
                ok = x_at + d < NX
                q_run = q_run + a_run * jnp.where(ok, bxr[NX - d - 1, m], 0.0)
                a_run = a_run * jnp.where(ok, fxr[NX - d - 1, m, 0], 1.0)
            qin[m] = qin[m] + zsuf[m] * q_run

        def grad_k(k, carry, g=g):
            gain = gain_ref[:, head_lanes(k)]
            v0 = vacc[0, k]
            v1 = vacc[1, k]
            v2 = vacc[2, k]
            for m in range(g * MG, (g + 1) * MG):
                seg = slice(m * 8, m * 8 + 8)
                prev = eh[k, seg, :] + ea[k, seg, :] * from_tile(stin, (m,), k)
                q = ebq[k, seg, :] + eba[k, seg, :] * from_tile(qin, (m,), k)
                terms = []
                for j in range(8):
                    at = slice(m * ROWS + j * 8, m * ROWS + j * 8 + 8)
                    t = dec[k, at, :] * prev
                    terms.append((t - rr[k, at, :]) * kk[k, at, :])
                    prev = t + drv[k, at, :]
                rate_rows, input_rows = [None] * 8, [None] * 8
                for j in range(7, -1, -1):
                    at = slice(m * ROWS + j * 8, m * ROWS + j * 8 + 8)
                    sg = upp[k, at, :] + q
                    q = dec[k, at, :] * sg
                    rate_rows[j] = sg * terms[j]
                    input_rows[j] = sg * cc[k, at, :]
                    dg[k, at, :] = sg * mi[k, at, :]
                gr = jnp.concatenate(rate_rows, axis=0).astype(BF16)
                gi = jnp.concatenate(input_rows, axis=0).astype(BF16)
                rows = slice(m * ROWS, (m + 1) * ROWS)
                gb[k, rows, :HEAD] = gr
                gb[k, rows, HEAD:] = gi
                v0 = v0 + jnp.sum(gr.astype(F32).reshape(8, 8, HEAD), axis=0)
                v1 = v1 + jnp.sum(gi.astype(F32).reshape(8, 8, HEAD), axis=0)
            grow = slice(g * GR, (g + 1) * GR)
            bp = dot_t(gb[k, grow, :HEAD], rwv[k]) + dot_t(gb[k, grow, HEAD:], iwv[k])
            for m in range(g * MG, (g + 1) * MG):
                rows = slice(m * ROWS, (m + 1) * ROWS)
                own = slice((m - g * MG) * ROWS, (m - g * MG + 1) * ROWS)
                gn = dg[k, rows, :] + bp[own]
                w = gn * xp[k, rows, :]
                v2 = v2 + jnp.sum((w * invb[m]).reshape(8, 8, HEAD), axis=0)
                wg = w * gain
                ca[m] += wg[:, :128] + wg[:, 128:]
                sv[k, rows, :] = upp[k, rows, :] + gn * gain * invb[m]
            vacc[0, k] = v0
            vacc[1, k] = v1
            vacc[2, k] = v2
            return carry

        lax.fori_loop(0, HEADS, grad_k, 0)
        tile = jnp.zeros((8, 128), F32)
        for m in range(g * MG, (g + 1) * MG):
            for j in range(8):
                col = jnp.sum(ca[m, j * 8 : j * 8 + 8, :], axis=1, keepdims=True)
                tile = jnp.where(lane_t == m * 8 + j, col, tile)
        s2[g] = tile
        for d in range(1, NY):
            s2_copy(g, d).start()

    def rx_copy(k, d):
        return remote(
            wgb.at[k, (x_at + d) % NX], rx.at[k, d - 1], rx_ss.at[k, d - 1], rx_rs.at[k, d - 1], x_peer(d)
        )

    for k in range(HEADS):
        w_k = dot(ndt[k], gb[k]).astype(BF16)
        for c in range(NX):
            for z in range(NZ):
                top = c * ROWS + (z // 2) * 16
                wgb[k, c, z] = w_k[top : top + 16, (z % 2) * HEAD : (z % 2) * HEAD + HEAD]
        for d in range(1, NX):
            rx_copy(k, d).start()

    def vz_copy(d):
        return remote(vzs, vzr.at[d - 1], vz_ss.at[d - 1], vz_rs.at[d - 1], z_peer(d))

    def vx_copy(d):
        return remote(vxs, vxr.at[d - 1], vx_ss.at[d - 1], vx_rs.at[d - 1], x_peer(d))

    for i in range(3):
        for k in range(HEADS):
            to_tile(vzs, (i,), k, jnp.sum(vacc[i, k], axis=0, keepdims=True))
    for d in range(1, NZ):
        vz_copy(d).start()

    outs = []
    for g in range(GROUPS):
        for d in range(1, NY):
            s2_copy(g, d).wait_recv()
        cross = s2[g] + s2r[g, 0] + s2r[g, 1] + s2r[g, 2]
        inv = inv_t[...]
        factor = cross * (inv * inv * inv) * (1.0 / FULL)
        for m in range(g * MG, (g + 1) * MG):
            for j in range(8):
                at = m * 8 + j
                fb[m, j * 8 : j * 8 + 8, :] = jnp.broadcast_to(factor[:, at : at + 1], (8, HEAD))
            rows = slice(m * ROWS, (m + 1) * ROWS)
            for k in range(HEADS):
                o = (sv[k, rows, :] - xp[k, rows, :] * fb[m]).astype(BF16)
                igv[m, :, k * HEAD : (k + 1) * HEAD] = dot(perm_back, o).astype(BF16)

        @pl.when(sec == 1)
        def _(g=g):
            up_copy(g).start()

        out = pltpu.make_async_copy(igv.at[group(g)], ig_hbm.at[group(g)], out_sem.at[g])
        out.start()
        outs.append(out)

    def rz_copy(k, d):
        return remote(
            rs1.at[k, (z_at + d) % NZ], rz.at[k, d - 1], rz_ss.at[k, d - 1], rz_rs.at[k, d - 1], z_peer(d)
        )

    def az_copy(k, d):
        own = wgo.at[k, x_at, z_at]
        return remote(own, own, az_ss.at[k, d - 1], az_rs.at[k, d - 1], z_peer(d))

    def az_arrival(k, d):
        own = wgo.at[k, x_at, (z_at + NZ - d) % NZ]
        return remote(own, own, az_ss.at[k, d - 1], az_rs.at[k, d - 1], z_peer(d))

    def ax_copy(k, d):
        own = wgo.at[k, x_at]
        return remote(own, own, ax_ss.at[k, d - 1], ax_rs.at[k, d - 1], x_peer(d))

    def ax_arrival(k, d):
        own = wgo.at[k, (x_at + NX - d) % NX]
        return remote(own, own, ax_ss.at[k, d - 1], ax_rs.at[k, d - 1], x_peer(d))

    for k in range(HEADS):
        for d in range(1, NX):
            rx_copy(k, d).wait_recv()
        total = wgb[k, x_at].astype(F32)
        for d in range(1, NX):
            total = total + rx[k, d - 1].astype(F32)
        rs1[k] = total.astype(BF16)
        for d in range(1, NZ):
            rz_copy(k, d).start()

    for d in range(1, NZ):
        vz_copy(d).wait_recv()
    v_sum = vzs[...]
    for d in range(1, NZ):
        v_sum = v_sum + vzr[d - 1]
    vxs[...] = v_sum
    for d in range(1, NX):
        vx_copy(d).start()

    for k in range(HEADS):
        for d in range(1, NZ):
            rz_copy(k, d).wait_recv()
        total = rs1[k, z_at].astype(F32)
        for d in range(1, NZ):
            total = total + rz[k, d - 1].astype(F32)
        wgo[k, x_at, z_at] = total.astype(BF16)
        for d in range(1, NZ):
            az_copy(k, d).start()

    for d in range(1, NX):
        vx_copy(d).wait_recv()
    v_sum = vxs[...]
    for d in range(1, NX):
        v_sum = v_sum + vxr[d - 1]
    vec_ref[...] = v_sum

    for k in range(HEADS):
        for d in range(1, NZ):
            az_arrival(k, d).wait_recv()
        for d in range(1, NX):
            ax_copy(k, d).start()
        out = pltpu.make_async_copy(wgo.at[k, x_at], wg_hbm.at[k, x_at], wout_sem.at[k, 0])
        out.start()
        outs.append(out)
    for k in range(HEADS):
        for d in range(1, NX):
            ax_arrival(k, d).wait_recv()
            at = (x_at + NX - d) % NX
            out = pltpu.make_async_copy(wgo.at[k, at], wg_hbm.at[k, at], wout_sem.at[k, d])
            out.start()
            outs.append(out)

    for c in s1_copies:
        c.wait_send()
    for g in range(GROUPS):
        for d in range(1, NZ):
            fz(g, d).wait_send()
            bz(g, d).wait_send()
        for d in range(1, NX):
            fx(g, d).wait_send()
            bx(g, d).wait_send()
        for d in range(1, NY):
            s2_copy(g, d).wait_send()

    @pl.when(sec == 1)
    def _():
        for g in range(GROUPS):
            up_copy(g).wait_send()

    for d in range(1, NZ):
        vz_copy(d).wait_send()
    for d in range(1, NX):
        vx_copy(d).wait_send()
    for k in range(HEADS):
        for d in range(1, NX):
            rx_copy(k, d).wait_send()
            ax_copy(k, d).wait_send()
        for d in range(1, NZ):
            rz_copy(k, d).wait_send()
            az_copy(k, d).wait_send()
    for out in outs:
        out.wait()


def on_device(
    layer_inputs, out_grad, rate_weight, input_weight, rate_bias, input_bias, decay_param, norm_gain, doc_starts
):
    tokens = MICRO * ROWS
    wide = pltpu.VMEM((HEADS, tokens, HEAD), F32)
    seg = pltpu.VMEM((HEADS, MICRO * 8, HEAD), F32)
    dma = pltpu.SemaphoreType.DMA

    def tiles(*lead, dtype=F32):
        return pltpu.VMEM((*lead, 8, 128), dtype)

    scratch = [
        pltpu.VMEM((MICRO, ROWS, WIDTH), BF16),
        pltpu.VMEM((MICRO, ROWS, WIDTH), BF16),
        pltpu.VMEM((HEADS, HEAD, HEAD), BF16),
        pltpu.VMEM((HEADS, HEAD, HEAD), BF16),
        wide,
        pltpu.VMEM((HEADS, tokens, HEAD), BF16),
        wide, wide, wide, wide, wide, wide,
        wide, wide, wide,
        pltpu.VMEM((HEADS, tokens, 2 * HEAD), BF16),
        pltpu.VMEM((MICRO, ROWS, HEAD), F32),
        pltpu.VMEM((MICRO, ROWS, HEAD), F32),
        tiles(),
        pltpu.VMEM((MICRO, ROWS, HEAD), F32),
        seg, seg, seg, seg, seg,
        tiles(MICRO, 2), tiles(NZ - 1, MICRO, 2),
        tiles(MICRO, 2), tiles(NX - 1, MICRO, 2),
        tiles(MICRO), tiles(NZ - 1, MICRO),
        tiles(MICRO), tiles(NX - 1, MICRO),
        tiles(MICRO), tiles(MICRO), tiles(MICRO, 2), tiles(MICRO),
        tiles(), tiles(NY - 1),
        pltpu.VMEM((MICRO, ROWS, 128), F32),
        tiles(GROUPS), tiles(GROUPS, NY - 1),
        pltpu.VMEM((MICRO, ROWS, WIDTH), BF16),
        pltpu.VMEM((3, HEADS, 8, HEAD), F32),
        tiles(3), tiles(NZ - 1, 3), tiles(3), tiles(NX - 1, 3),
        pltpu.VMEM((HEADS, HEAD, tokens), BF16),
        pltpu.VMEM((HEADS, NX, NZ, 16, HEAD), BF16),
        pltpu.VMEM((HEADS, NX - 1, NZ, 16, HEAD), BF16),
        pltpu.VMEM((HEADS, NZ, 16, HEAD), BF16),
        pltpu.VMEM((HEADS, NZ - 1, 16, HEAD), BF16),
        pltpu.VMEM((HEADS, NX, NZ, 16, HEAD), BF16),
        dma((4,)), dma((GROUPS,)), dma((HEADS, NX)),
    ]
    scratch += [dma((NY - 1,))] * 2 + [dma((GROUPS, NY - 1))] * 2
    scratch += ([dma((GROUPS, NZ - 1))] * 2 + [dma((GROUPS, NX - 1))] * 2) * 2
    scratch += [dma((GROUPS,))] * 2
    scratch += [dma((NZ - 1,))] * 2 + [dma((NX - 1,))] * 2
    scratch += [dma((HEADS, NX - 1))] * 2 + [dma((HEADS, NZ - 1))] * 4 + [dma((HEADS, NX - 1))] * 2

    hbm = pl.BlockSpec(memory_space=pl.ANY)
    vmem = pl.BlockSpec(memory_space=pltpu.VMEM)
    input_grads, weight_sums, vector_sums = pl.pallas_call(
        body,
        out_shape=(
            jax.ShapeDtypeStruct((MICRO, ROWS, WIDTH), BF16),
            jax.ShapeDtypeStruct((HEADS, NX, NZ, 16, HEAD), BF16),
            jax.ShapeDtypeStruct((3, 8, 128), F32),
        ),
        in_specs=[hbm] * 4 + [vmem] * 4 + [pl.BlockSpec(memory_space=pltpu.SMEM)],
        out_specs=(hbm, hbm, vmem),
        scratch_shapes=scratch,
        compiler_params=pltpu.CompilerParams(
            collective_id=0, has_side_effects=True, vmem_limit_bytes=48 << 20
        ),
        name="rglru_backward",
    )(layer_inputs, out_grad, rate_weight, input_weight, rate_bias, input_bias, decay_param, norm_gain, doc_starts)
    scale = 1.0 / math.sqrt(MICRO * ROWS * NX * NZ)
    pairs = weight_sums.reshape(HEADS, HEAD // 16, 2, 16, HEAD)
    rate_grad = (pairs[:, :, 0].astype(F32) * scale).reshape(1, HEADS, HEAD, HEAD)
    input_grad = (pairs[:, :, 1].astype(F32) * scale).reshape(1, HEADS, HEAD, HEAD)
    return (input_grads[None], rate_grad, input_grad, (vector_sums * scale).reshape(1, 3, WIDTH))


def solution(mesh):
    in_specs = (
        P("section", None, "seq", "chan"),
        P(None, "seq", "chan"),
        P("section", "chan", None, None),
        P("section", "chan", None, None),
        P("section", "chan"),
        P("section", "chan"),
        P("section", "chan"),
        P("section", "chan"),
        P(),
    )
    out_specs = (
        P("section", None, "seq", "chan"),
        P("section", "chan", None, None),
        P("section", "chan", None, None),
        P("section", None, "chan"),
    )
    return jax.shard_map(
        on_device, mesh=mesh, in_specs=in_specs, out_specs=out_specs, check_vma=False
    )
```

```python
import math

import jax
import jax.numpy as jnp
from jax import lax
from jax.experimental import pallas as pl
from jax.experimental.pallas import tpu as pltpu
from jax.sharding import PartitionSpec as P

F32 = jnp.float32
BF16 = jnp.bfloat16
NX, NZ, NY = 4, 8, 4
MICRO, ROWS, WIDTH = 4, 64, 1024
HEADS, HEAD = 4, 256
FULL = WIDTH * NY
GROUPS = 2
MG = MICRO // GROUPS
GR = MG * ROWS
MESH = pl.DeviceIdType.MESH
FAR_Z = (4, 3, 5, 2, 6, 1, 7)
FAR_4 = (2, 1, 3)


def dot(a, b):
    return jnp.dot(a, b, preferred_element_type=F32)


def dot_t(a, b):
    return lax.dot_general(a, b, (((1,), (1,)), ((), ())), preferred_element_type=F32)


def sublane(shape):
    return lax.broadcasted_iota(jnp.int32, shape, 0)


def lane(shape):
    return lax.broadcasted_iota(jnp.int32, shape, 1)


def log1p_of(v):
    series = v * (1.0 - v * (0.5 - v * (1.0 / 3.0 - v * (0.25 - v * 0.2))))
    return jnp.where(v < 0.03125, series, jnp.log(1.0 + v))


def log_of(a):
    return jnp.log(jnp.maximum(a, 1e-37))


def decay_of(tile):
    wide = tile.astype(F32)
    return jnp.where(wide < -80.0, 0.0, jnp.exp(wide))


def body(
    x_hbm, up_hbm, rw_hbm, iw_hbm, rb_hbm, ib_hbm, dp_hbm, gain_hbm, starts_hbm,
    igv, wgo, vec_ref,
    rb_ref, ib_ref, dp_ref, gain_ref, starts_ref,
    xv, upv, rwv, iwv, xp, nd, dec, drv, mi, rr, kk, cc, upp, sv, dg, gb, keep, invb, inv_t, fb,
    ea, eh, eba, ebq, pa_s, fzt, bzt, za, fzs, fzr, fxs, fxr, bzs, bzr, bxs, bxr, stin, qin, zpre, zsuf,
    s1, s1r, ca, s2, s2r, vacc, vzs, vzr, vxs, vxr,
    ndt, wgb, rx, rs1, rz,
    loc_sem, s1_ss, s1_rs, s2_ss, s2_rs, fz_ss, fz_rs, fx_ss, fx_rs, bz_ss, bz_rs, bx_ss, bx_rs,
    up_ss, up_rs, vz_ss, vz_rs, vx_ss, vx_rs, rx_ss, rx_rs, rz_ss, rz_rs, az_ss, az_rs, ax_ss, ax_rs, gate,
):
    sec = lax.axis_index("section")
    seq = lax.axis_index("seq")
    chan = lax.axis_index("chan")
    x_at = seq // NZ
    z_at = seq % NZ

    def z_peer(d):
        return {"seq": x_at * NZ + (z_at + d) % NZ}

    def x_peer(d):
        return {"seq": ((x_at + d) % NX) * NZ + z_at}

    def y_peer(d):
        return {"chan": (chan + d) % NY}

    other_core = {"section": 1 - sec}

    def remote(src, dst, ss, rs, to):
        return pltpu.make_async_remote_copy(
            src_ref=src, dst_ref=dst, send_sem=ss, recv_sem=rs, device_id=to, device_id_type=MESH
        )

    loads = [
        pltpu.make_async_copy(x_hbm.at[0], xv, loc_sem.at[0]),
        pltpu.make_async_copy(starts_hbm, starts_ref, loc_sem.at[4]),
    ]
    w_loads = [
        pltpu.make_async_copy(gain_hbm, gain_ref, loc_sem.at[5]),
        pltpu.make_async_copy(dp_hbm, dp_ref, loc_sem.at[6]),
        pltpu.make_async_copy(rb_hbm, rb_ref, loc_sem.at[7]),
        pltpu.make_async_copy(ib_hbm, ib_ref, loc_sem.at[8]),
        pltpu.make_async_copy(rw_hbm.at[0], rwv, loc_sem.at[1]),
        pltpu.make_async_copy(iw_hbm.at[0], iwv, loc_sem.at[2]),
    ]
    up_load = pltpu.make_async_copy(up_hbm, upv, loc_sem.at[3])
    for c in loads + w_loads:
        c.start()

    @pl.when(sec == 1)
    def _():
        up_load.start()

    barrier = pltpu.get_barrier_semaphore()
    peers = [z_peer(d) for d in range(1, NZ)] + [x_peer(d) for d in range(1, NX)]
    peers += [y_peer(d) for d in range(1, NY)] + [other_core]
    for to in peers:
        pl.semaphore_signal(barrier, inc=1, device_id=to, device_id_type=MESH)

    r_i = sublane((ROWS, ROWS))
    t_i = lane((ROWS, ROWS))
    perm = jnp.where(t_i == (r_i % 8) * 8 + r_i // 8, 1.0, 0.0).astype(BF16)
    perm_back = jnp.where(r_i == (t_i % 8) * 8 + t_i // 8, 1.0, 0.0).astype(BF16)

    vacc[...] = jnp.zeros_like(vacc)
    ca[...] = jnp.zeros_like(ca)


    for c in loads:
        c.wait()
    lane_t = lane((8, 128))
    tile = jnp.zeros((8, 128), F32)
    for m in range(MICRO):
        x_m = dot(perm, xv[m])
        acc = jnp.zeros((ROWS, 128), F32)
        for k in range(HEADS):
            x_k = x_m[:, k * HEAD : (k + 1) * HEAD]
            xp[k, m * ROWS : (m + 1) * ROWS, :] = x_k
            sq = x_k * x_k
            acc = acc + (sq[:, :128] + sq[:, 128:])
        for j in range(8):
            col = jnp.sum(acc[j * 8 : j * 8 + 8], axis=1, keepdims=True)
            tile = jnp.where(lane_t == m * 8 + j, col, tile)
    s1[...] = tile
    pl.semaphore_wait(barrier, len(peers))
    s1_copies = [
        remote(s1, s1r.at[d - 1], s1_ss.at[d - 1], s1_rs.at[d - 1], y_peer(d)) for d in range(1, NY)
    ]
    for c in s1_copies:
        c.start()
    r_w = sublane((ROWS, HEAD))
    position = seq * ROWS + (r_w % 8) * 8 + r_w // 8
    for m in range(MICRO):
        reset = position == 0
        for d in range(3):
            reset = jnp.logical_or(reset, position == starts_ref[m, d])
        keep[m] = jnp.where(reset, 0.0, 1.0)
    for c in w_loads:
        c.wait()
    for c in s1_copies:
        c.wait_recv()
    inv_tile = lax.rsqrt((s1[...] + s1r[0] + s1r[1] + s1r[2]) / FULL + 1e-06)
    inv_t[...] = inv_tile
    for m in range(MICRO):
        for j in range(8):
            at = m * 8 + j
            invb[m, j * 8 : j * 8 + 8, :] = jnp.broadcast_to(inv_tile[:, at : at + 1], (8, HEAD))

    sub = sublane((8, HEAD))

    def scan_up(a, h):
        for sh in (1, 2, 4):
            ok = sub >= sh
            h = h + a * jnp.where(ok, pltpu.roll(h, sh, 0), 0.0)
            a = a * jnp.where(ok, pltpu.roll(a, sh, 0), 1.0)
        return a, h

    def scan_down(a, h):
        for sh in (1, 2, 4):
            ok = sub < 8 - sh
            h = h + a * jnp.where(ok, pltpu.roll(h, 8 - sh, 0), 0.0)
            a = a * jnp.where(ok, pltpu.roll(a, 8 - sh, 0), 1.0)
        return a, h

    def to_tile(ref, index, k, row):
        for half in range(2):
            ref[(*index, pl.ds(k * 2 + half, 1), slice(None))] = row[:, half * 128 : half * 128 + 128]

    def from_tile(ref, index, k):
        return jnp.concatenate(
            [ref[(*index, pl.ds(k * 2 + half, 1), slice(None))] for half in range(2)], axis=1
        )

    def head_lanes(k):
        return pl.ds(pl.multiple_of(k * HEAD, HEAD), HEAD)

    def forward_head(g, k):
        gain = gain_ref[:, head_lanes(k)]
        rb = rb_ref[:, head_lanes(k)]
        ib = ib_ref[:, head_lanes(k)]
        v = dp_ref[:, head_lanes(k)]
        rate = -8.0 * (jnp.maximum(-v, 0.0) + log1p_of(jnp.exp(-jnp.abs(v))))
        for m in range(g * MG, (g + 1) * MG):
            rows = slice(m * ROWS, (m + 1) * ROWS)
            nd[k, rows, :] = (xp[k, rows, :] * invb[m] * gain).astype(BF16)
        grow = slice(g * GR, (g + 1) * GR)
        n_g = nd[k, grow, :]
        pre_r = dot(n_g, rwv[k])
        pre_i = dot(n_g, iwv[k])
        for m in range(g * MG, (g + 1) * MG):
            rows = slice(m * ROWS, (m + 1) * ROWS)
            own = slice((m - g * MG) * ROWS, (m - g * MG + 1) * ROWS)
            rg = 0.5 * jnp.tanh(0.5 * (pre_r[own] + rb)) + 0.5
            ig = 0.5 * jnp.tanh(0.5 * (pre_i[own] + ib)) + 0.5
            nw = n_g[own].astype(F32)
            kept = keep[m]
            ld = rate * rg
            e = jnp.exp(ld)
            gap = e * e
            u = ld + ld
            series = -u * (1.0 + u * (0.5 + u * (1.0 / 6.0 + u * (1.0 / 24.0 + u * (1.0 / 120.0)))))
            em = jnp.where(u > -0.125, series, 1.0 - gap)
            em = jnp.maximum(em, 1e-06)
            rs = lax.rsqrt(em)
            mult = jnp.where(kept > 0.5, em * rs, 1.0)
            a = e * kept
            mig = mult * ig
            b = mig * nw
            dec[k, rows, :] = a
            drv[k, rows, :] = b
            mi[k, rows, :] = mig
            rr[k, rows, :] = kept * (ig * nw * gap * rs)
            kk[k, rows, :] = ld * (1.0 - rg)
            cc[k, rows, :] = b * (1.0 - ig)
            pa = a[:8]
            h = b[:8]
            for j in range(1, 8):
                a_j = a[j * 8 : j * 8 + 8]
                h = a_j * h + b[j * 8 : j * 8 + 8]
                pa = pa * a_j
            seg = slice(m * 8, m * 8 + 8)
            pa_s[k, seg, :] = pa
            a_in, h_in = scan_up(pa, h)
            ea[k, seg, :] = jnp.where(sub >= 1, pltpu.roll(a_in, 1, 0), 1.0)
            eh[k, seg, :] = jnp.where(sub >= 1, pltpu.roll(h_in, 1, 0), 0.0)
            to_tile(fzt, (m, 0), k, a_in[7:8])
            to_tile(fzt, (m, 1), k, h_in[7:8])

    def group(g):
        return pl.ds(g * MG, MG)

    def fz(g, d):
        return remote(
            fzs.at[group(g)], fzr.at[d - 1, group(g)], fz_ss.at[g, d - 1], fz_rs.at[g, d - 1], z_peer(d)
        )

    def fx(g, d):
        return remote(
            fxs.at[group(g)], fxr.at[d - 1, group(g)], fx_ss.at[g, d - 1], fx_rs.at[g, d - 1], x_peer(d)
        )

    def bz(g, d):
        return remote(
            bzs.at[group(g)], bzr.at[d - 1, group(g)], bz_ss.at[g, d - 1], bz_rs.at[g, d - 1], z_peer(d)
        )

    def bx(g, d):
        return remote(
            bxs.at[group(g)], bxr.at[d - 1, group(g)], bx_ss.at[g, d - 1], bx_rs.at[g, d - 1], x_peer(d)
        )

    def back_local(g):
        for m in range(g * MG, (g + 1) * MG):
            u_m = dot(perm, upv[m])
            for k in range(HEADS):
                upp[k, m * ROWS : (m + 1) * ROWS, :] = u_m[:, k * HEAD : (k + 1) * HEAD]

        for k in range(HEADS):
            for m in range(g * MG, (g + 1) * MG):
                q = jnp.zeros((8, HEAD), F32)
                for j in range(7, -1, -1):
                    at = slice(m * ROWS + j * 8, m * ROWS + j * 8 + 8)
                    q = dec[k, at, :] * (upp[k, at, :] + q)
                seg = slice(m * 8, m * 8 + 8)
                a_in, q_in = scan_down(pa_s[k, seg, :], q)
                eba[k, seg, :] = jnp.where(sub < 7, pltpu.roll(a_in, 7, 0), 1.0)
                ebq[k, seg, :] = jnp.where(sub < 7, pltpu.roll(q_in, 7, 0), 0.0)
                to_tile(bzt, (m,), k, q_in[0:1])
        for m in range(g * MG, (g + 1) * MG):
            bzs[m] = bzt[m].astype(BF16)
        for d in FAR_Z:
            bz(g, d).start()

    @pl.when(sec == 1)
    def _():
        up_load.wait()

    for g in range(GROUPS):
        for k in range(HEADS):
            forward_head(g, k)
        for m in range(g * MG, (g + 1) * MG):
            fzs[m, 0] = log_of(fzt[m, 0]).astype(BF16)
            fzs[m, 1] = fzt[m, 1].astype(BF16)
        for d in FAR_Z:
            fz(g, d).start()

        @pl.when(sec == 1)
        def _(g=g):
            back_local(g)

    def turn_k(k, carry):
        ndt[k] = nd[k].T
        return carry

    lax.fori_loop(0, HEADS, turn_k, 0)

    def forward_totals(g):
        for d in range(1, NZ):
            fz(g, d).wait_recv()
        for m in range(g * MG, (g + 1) * MG):
            a_own, h_own = fzt[m, 0], fzt[m, 1]
            a_pre, h_pre = jnp.ones((8, 128), F32), jnp.zeros((8, 128), F32)
            a_suf, h_suf = a_pre, h_pre
            for d in range(1, NZ):
                ok = z_at >= d
                h_pre = h_pre + a_pre * jnp.where(ok, fzr[d - 1, m, 1].astype(F32), 0.0)
                a_d = decay_of(fzr[d - 1, m, 0])
                za[d - 1, m] = a_d
                a_pre = a_pre * jnp.where(ok, a_d, 1.0)
            for d in range(1, NZ):
                ok = z_at + d < NZ
                a_d = jnp.where(ok, za[NZ - d - 1, m], 1.0)
                h_suf = jnp.where(ok, fzr[NZ - d - 1, m, 1].astype(F32), 0.0) + a_d * h_suf
                a_suf = a_suf * a_d
            zpre[m, 0] = a_pre
            zpre[m, 1] = h_pre
            zsuf[m] = a_suf
            fxs[m, 0] = log_of(a_pre * a_own * a_suf).astype(BF16)
            fxs[m, 1] = (h_suf + a_suf * (h_own + a_own * h_pre)).astype(BF16)
        for d in FAR_4:
            fx(g, d).start()

    def up_copy(g):
        return remote(igv.at[group(g)], upv.at[group(g)], up_ss.at[g], up_rs.at[g], other_core)

    def backward_totals(g):
        for d in range(1, NZ):
            bz(g, d).wait_recv()
        for m in range(g * MG, (g + 1) * MG):
            a_run, q_run = jnp.ones((8, 128), F32), jnp.zeros((8, 128), F32)
            for d in range(1, NZ):
                ok = z_at + d < NZ
                q_run = q_run + a_run * jnp.where(ok, bzr[NZ - d - 1, m].astype(F32), 0.0)
                a_run = a_run * jnp.where(ok, za[NZ - d - 1, m], 1.0)
            qin[m] = q_run
            total = bzt[m] + fzt[m, 0] * q_run
            for d in range(1, NZ):
                ok = z_at >= d
                total = jnp.where(ok, bzr[d - 1, m].astype(F32) + za[d - 1, m] * total, total)
            bxs[m] = total.astype(BF16)
        for d in FAR_4:
            bx(g, d).start()

    def state_carry(g):
        for d in range(1, NX):
            fx(g, d).wait_recv()
        for m in range(g * MG, (g + 1) * MG):
            a_run, h_run = jnp.ones((8, 128), F32), jnp.zeros((8, 128), F32)
            for d in range(1, NX):
                ok = x_at >= d
                h_run = h_run + a_run * jnp.where(ok, fxr[d - 1, m, 1].astype(F32), 0.0)
                a_run = a_run * jnp.where(ok, decay_of(fxr[d - 1, m, 0]), 1.0)
            stin[m] = zpre[m, 1] + zpre[m, 0] * h_run

    for g in range(GROUPS):
        forward_totals(g)

        @pl.when(sec == 1)
        def _(g=g):
            backward_totals(g)

    @pl.when(sec == 0)
    def _():
        for g in range(GROUPS):
            state_carry(g)
        for g in range(GROUPS):
            up_copy(g).wait_recv()
            back_local(g)

    @pl.when(sec == 0)
    def _():
        for g in range(GROUPS):
            backward_totals(g)

    def s2_copy(g, d):
        return remote(s2.at[g], s2r.at[g, d - 1], s2_ss.at[g, d - 1], s2_rs.at[g, d - 1], y_peer(d))

    def q_carry(g):
        for d in range(1, NX):
            bx(g, d).wait_recv()
        for m in range(g * MG, (g + 1) * MG):
            a_run, q_run = jnp.ones((8, 128), F32), jnp.zeros((8, 128), F32)
            for d in range(1, NX):
                ok = x_at + d < NX
                q_run = q_run + a_run * jnp.where(ok, bxr[NX - d - 1, m].astype(F32), 0.0)
                a_run = a_run * jnp.where(ok, decay_of(fxr[NX - d - 1, m, 0]), 1.0)
            qin[m] = qin[m] + zsuf[m] * q_run

    def grad_head(k, low, high):
        gain = gain_ref[:, head_lanes(k)]
        v0 = vacc[0, k]
        v1 = vacc[1, k]
        v2 = vacc[2, k]
        for m in range(low, high):
            seg = slice(m * 8, m * 8 + 8)
            prev = eh[k, seg, :] + ea[k, seg, :] * from_tile(stin, (m,), k)
            q = ebq[k, seg, :] + eba[k, seg, :] * from_tile(qin, (m,), k)
            terms = []
            for j in range(8):
                at = slice(m * ROWS + j * 8, m * ROWS + j * 8 + 8)
                t = dec[k, at, :] * prev
                terms.append((t - rr[k, at, :]) * kk[k, at, :])
                prev = t + drv[k, at, :]
            rate_rows, input_rows = [None] * 8, [None] * 8
            for j in range(7, -1, -1):
                at = slice(m * ROWS + j * 8, m * ROWS + j * 8 + 8)
                sg = upp[k, at, :] + q
                q = dec[k, at, :] * sg
                rate_rows[j] = sg * terms[j]
                input_rows[j] = sg * cc[k, at, :]
                dg[k, at, :] = sg * mi[k, at, :]
            gr = jnp.concatenate(rate_rows, axis=0).astype(BF16)
            gi = jnp.concatenate(input_rows, axis=0).astype(BF16)
            rows = slice(m * ROWS, (m + 1) * ROWS)
            gb[k, rows, :HEAD] = gr
            gb[k, rows, HEAD:] = gi
            v0 = v0 + jnp.sum(gr.astype(F32).reshape(8, 8, HEAD), axis=0)
            v1 = v1 + jnp.sum(gi.astype(F32).reshape(8, 8, HEAD), axis=0)
        grow = slice(low * ROWS, high * ROWS)
        bp = dot_t(gb[k, grow, :HEAD], rwv[k]) + dot_t(gb[k, grow, HEAD:], iwv[k])
        for m in range(low, high):
            rows = slice(m * ROWS, (m + 1) * ROWS)
            own = slice((m - low) * ROWS, (m - low + 1) * ROWS)
            gn = dg[k, rows, :] + bp[own]
            w = gn * xp[k, rows, :]
            v2 = v2 + jnp.sum((w * invb[m]).reshape(8, 8, HEAD), axis=0)
            wg = w * gain
            ca[m] += wg[:, :128] + wg[:, 128:]
            sv[k, rows, :] = upp[k, rows, :] + gn * gain * invb[m]
        vacc[0, k] = v0
        vacc[1, k] = v1
        vacc[2, k] = v2

    def cross_sums(g):
        tile = jnp.zeros((8, 128), F32)
        for m in range(g * MG, (g + 1) * MG):
            for j in range(8):
                col = jnp.sum(ca[m, j * 8 : j * 8 + 8, :], axis=1, keepdims=True)
                tile = jnp.where(lane_t == m * 8 + j, col, tile)
        s2[g] = tile
        for d in FAR_4:
            s2_copy(g, d).start()

    def rx_copy(k, d):
        return remote(
            wgb.at[k, (x_at + d) % NX], rx.at[k, d - 1], rx_ss.at[k, d - 1], rx_rs.at[k, d - 1], x_peer(d)
        )

    def weight_head(k):
        w_k = dot(ndt[k], gb[k]).astype(BF16)
        for c in range(NX):
            for z in range(NZ):
                top = c * ROWS + (z // 2) * 16
                wgb[k, c, z] = w_k[top : top + 16, (z % 2) * HEAD : (z % 2) * HEAD + HEAD]
        for d in FAR_4:
            rx_copy(k, d).start()

    def rz_copy(k, d):
        return remote(
            rs1.at[k, (z_at + d) % NZ], rz.at[k, d - 1], rz_ss.at[k, d - 1], rz_rs.at[k, d - 1], z_peer(d)
        )

    def piece(x, z, p):
        return wgo.at[x, z, pl.ds(p * 2, 2)]

    def from_z(d):
        return (z_at + NZ - d) % NZ

    def az_copy(p, d, arrival=False):
        ref = piece(x_at, from_z(d) if arrival else z_at, p)
        return remote(ref, ref, az_ss.at[p, d - 1], az_rs.at[p, d - 1], z_peer(d))

    def ax_copy(p, e, d, arrival=False):
        ref = piece((x_at + NX - e) % NX if arrival else x_at, from_z(d), p)
        return remote(ref, ref, ax_ss.at[p, e - 1, d], ax_rs.at[p, e - 1, d], x_peer(e))

    def spread(p, d):
        if d:
            az_copy(p, d, True).wait_recv()
        for e in FAR_4:
            ax_copy(p, e, d).start()

    def own_head(k):
        for d in range(1, NX):
            rx_copy(k, d).wait_recv()
        total = wgb[k, x_at].astype(F32)
        for d in range(1, NX):
            total = total + rx[k, d - 1].astype(F32)
        rs1[k] = total.astype(BF16)
        for d in FAR_Z:
            rz_copy(k, d).start()

    def vz_copy(d):
        return remote(vzs, vzr.at[d - 1], vz_ss.at[d - 1], vz_rs.at[d - 1], z_peer(d))

    def vx_copy(d):
        return remote(vxs, vxr.at[d - 1], vx_ss.at[d - 1], vx_rs.at[d - 1], x_peer(d))

    def vector_sums():
        for i in range(3):
            for k in range(HEADS):
                to_tile(vzs, (i,), k, jnp.sum(vacc[i, k], axis=0, keepdims=True))
        for d in FAR_Z:
            vz_copy(d).start()

    def finish_inputs(g):
        for d in range(1, NY):
            s2_copy(g, d).wait_recv()
        cross = s2[g] + s2r[g, 0] + s2r[g, 1] + s2r[g, 2]
        inv = inv_t[...]
        factor = cross * (inv * inv * inv) * (1.0 / FULL)
        for m in range(g * MG, (g + 1) * MG):
            for j in range(8):
                at = m * 8 + j
                fb[m, j * 8 : j * 8 + 8, :] = jnp.broadcast_to(factor[:, at : at + 1], (8, HEAD))
            rows = slice(m * ROWS, (m + 1) * ROWS)
            for k in range(HEADS):
                o = (sv[k, rows, :] - xp[k, rows, :] * fb[m]).astype(BF16)
                igv[m, :, k * HEAD : (k + 1) * HEAD] = dot(perm_back, o).astype(BF16)

    @pl.when(sec == 1)
    def _():
        for g in range(GROUPS):
            state_carry(g)
            q_carry(g)
            for k in range(HEADS):
                grad_head(k, g * MG, (g + 1) * MG)
            cross_sums(g)
        for k in range(HEADS):
            weight_head(k)

    @pl.when(sec == 0)
    def _():
        for g in range(GROUPS):
            q_carry(g)
        for k in range(HEADS):
            grad_head(k, 0, MICRO)
            weight_head(k)
        for g in range(GROUPS):
            cross_sums(g)

    vector_sums()

    @pl.when(sec == 1)
    def _():
        for g in range(GROUPS):
            finish_inputs(g)
            up_copy(g).start()

    for k in range(HEADS):
        own_head(k)

    @pl.when(sec == 0)
    def _():
        pl.semaphore_signal(gate, inc=1, device_id=other_core, device_id_type=MESH)
        for g in range(GROUPS):
            finish_inputs(g)

    for d in range(1, NZ):
        vz_copy(d).wait_recv()
    v_sum = vzs[...]
    for d in range(1, NZ):
        v_sum = v_sum + vzr[d - 1]
    vxs[...] = v_sum
    for d in FAR_4:
        vx_copy(d).start()

    for k in range(HEADS):
        for d in range(1, NZ):
            rz_copy(k, d).wait_recv()
        total = rs1[k, z_at].astype(F32)
        for d in range(1, NZ):
            total = total + rz[k, d - 1].astype(F32)
        wgo[x_at, z_at, k] = total.astype(BF16)
        if k % 2:
            for d in FAR_Z:
                az_copy(k // 2, d).start()

    @pl.when(sec == 1)
    def _():
        pl.semaphore_wait(gate, 1)

    for p in range(2):
        spread(p, 0)
    for near in ((1, 7), (2, 6), (3, 5)):
        for p in range(2):
            for d in near:
                spread(p, d)

    for p in range(2):
        spread(p, 4)

    for d in range(1, NX):
        vx_copy(d).wait_recv()
    v_sum = vxs[...]
    for d in range(1, NX):
        v_sum = v_sum + vxr[d - 1]
    vec_ref[...] = v_sum

    for p in range(2):
        for d in range(NZ):
            for e in range(1, NX):
                ax_copy(p, e, d, True).wait_recv()

    for c in s1_copies:
        c.wait_send()
    for g in range(GROUPS):
        for d in range(1, NZ):
            fz(g, d).wait_send()
            bz(g, d).wait_send()
        for d in range(1, NX):
            fx(g, d).wait_send()
            bx(g, d).wait_send()
        for d in range(1, NY):
            s2_copy(g, d).wait_send()

    @pl.when(sec == 1)
    def _():
        for g in range(GROUPS):
            up_copy(g).wait_send()

    for d in range(1, NZ):
        vz_copy(d).wait_send()
    for d in range(1, NX):
        vx_copy(d).wait_send()
    for k in range(HEADS):
        for d in range(1, NX):
            rx_copy(k, d).wait_send()
        for d in range(1, NZ):
            rz_copy(k, d).wait_send()
    for p in range(2):
        for d in range(1, NZ):
            az_copy(p, d).wait_send()
        for d in range(NZ):
            for e in range(1, NX):
                ax_copy(p, e, d).wait_send()


def hand_out(ig_ref, w_ref, v_ref, ig_out, rate_out, input_out, v_out, staged, v_staged, sem):
    scale = 1.0 / math.sqrt(MICRO * ROWS * NX * NZ)
    copies = [pltpu.make_async_copy(ig_ref, ig_out.at[0], sem.at[0])]
    copies[0].start()
    v_staged[...] = v_ref[...] * scale
    copies.append(pltpu.make_async_copy(v_staged, v_out, sem.at[1]))
    copies[1].start()
    for k in range(HEADS):
        for c in range(NX):
            for z in range(NZ):
                top = c * ROWS + (z // 2) * 16
                staged[z % 2, k, top : top + 16, :] = w_ref[c, z, k].astype(F32) * scale
        for half, out in enumerate((rate_out, input_out)):
            copies.append(pltpu.make_async_copy(staged.at[half, k], out.at[0, k], sem.at[2 + 2 * k + half]))
            copies[-1].start()
    for c in copies:
        c.wait()


def on_device(*arguments):
    tokens = MICRO * ROWS
    wide = pltpu.VMEM((HEADS, tokens, HEAD), F32)
    seg = pltpu.VMEM((HEADS, MICRO * 8, HEAD), F32)
    dma = pltpu.SemaphoreType.DMA

    def tiles(*lead, dtype=F32):
        return pltpu.VMEM((*lead, 8, 128), dtype)

    row = pltpu.VMEM((1, WIDTH), F32)
    scratch = [
        row, row, row, row, pltpu.SMEM((MICRO, 3), jnp.int32),
        pltpu.VMEM((MICRO, ROWS, WIDTH), BF16),
        pltpu.VMEM((MICRO, ROWS, WIDTH), BF16),
        pltpu.VMEM((HEADS, HEAD, HEAD), BF16),
        pltpu.VMEM((HEADS, HEAD, HEAD), BF16),
        wide,
        pltpu.VMEM((HEADS, tokens, HEAD), BF16),
        wide, wide, wide, wide, wide, wide,
        wide, wide, wide,
        pltpu.VMEM((HEADS, tokens, 2 * HEAD), BF16),
        pltpu.VMEM((MICRO, ROWS, HEAD), F32),
        pltpu.VMEM((MICRO, ROWS, HEAD), F32),
        tiles(),
        pltpu.VMEM((MICRO, ROWS, HEAD), F32),
        seg, seg, seg, seg, seg,
        tiles(MICRO, 2), tiles(MICRO), tiles(NZ - 1, MICRO),
        tiles(MICRO, 2, dtype=BF16), tiles(NZ - 1, MICRO, 2, dtype=BF16),
        tiles(MICRO, 2, dtype=BF16), tiles(NX - 1, MICRO, 2, dtype=BF16),
        tiles(MICRO, dtype=BF16), tiles(NZ - 1, MICRO, dtype=BF16),
        tiles(MICRO, dtype=BF16), tiles(NX - 1, MICRO, dtype=BF16),
        tiles(MICRO), tiles(MICRO), tiles(MICRO, 2), tiles(MICRO),
        tiles(), tiles(NY - 1),
        pltpu.VMEM((MICRO, ROWS, 128), F32),
        tiles(GROUPS), tiles(GROUPS, NY - 1),
        pltpu.VMEM((3, HEADS, 8, HEAD), F32),
        tiles(3), tiles(NZ - 1, 3), tiles(3), tiles(NX - 1, 3),
        pltpu.VMEM((HEADS, HEAD, tokens), BF16),
        pltpu.VMEM((HEADS, NX, NZ, 16, HEAD), BF16),
        pltpu.VMEM((HEADS, NX - 1, NZ, 16, HEAD), BF16),
        pltpu.VMEM((HEADS, NZ, 16, HEAD), BF16),
        pltpu.VMEM((HEADS, NZ - 1, 16, HEAD), BF16),
        dma((9,)),
    ]
    scratch += [dma((NY - 1,))] * 2 + [dma((GROUPS, NY - 1))] * 2
    scratch += ([dma((GROUPS, NZ - 1))] * 2 + [dma((GROUPS, NX - 1))] * 2) * 2
    scratch += [dma((GROUPS,))] * 2
    scratch += [dma((NZ - 1,))] * 2 + [dma((NX - 1,))] * 2
    scratch += [dma((HEADS, NX - 1))] * 2 + [dma((HEADS, NZ - 1))] * 2 + [dma((2, NZ - 1))] * 2
    scratch += [dma((2, NX - 1, NZ))] * 2 + [pltpu.SemaphoreType.REGULAR]

    hbm = pl.BlockSpec(memory_space=pltpu.HBM)
    vmem = pl.BlockSpec(memory_space=pltpu.VMEM)
    input_grads, weight_sums, vector_sums = pl.pallas_call(
        body,
        out_shape=(
            jax.ShapeDtypeStruct((MICRO, ROWS, WIDTH), BF16),
            jax.ShapeDtypeStruct((NX, NZ, HEADS, 16, HEAD), BF16),
            jax.ShapeDtypeStruct((3, 8, 128), F32),
        ),
        in_specs=[hbm] * 9,
        out_specs=(vmem, vmem, vmem),
        scratch_shapes=scratch,
        compiler_params=pltpu.CompilerParams(
            collective_id=0, has_side_effects=True, vmem_limit_bytes=48 << 20
        ),
        name="rglru_backward",
    )(*(pltpu.with_memory_space_constraint(v, pltpu.HBM) for v in arguments))
    square = jax.ShapeDtypeStruct((1, HEADS, HEAD, HEAD), F32)
    input_grads, rate_grad, input_grad, vector_grads = pl.pallas_call(
        hand_out,
        out_shape=(
            jax.ShapeDtypeStruct((1, MICRO, ROWS, WIDTH), BF16), square, square,
            jax.ShapeDtypeStruct((3, 8, 128), F32),
        ),
        in_specs=[vmem] * 3,
        out_specs=(hbm, hbm, hbm, hbm),
        scratch_shapes=[
            pltpu.VMEM((2, HEADS, HEAD, HEAD), F32), pltpu.VMEM((3, 8, 128), F32), dma((2 + 2 * HEADS,)),
        ],
        compiler_params=pltpu.CompilerParams(vmem_limit_bytes=8 << 20),
        name="hand_out",
    )(input_grads, weight_sums, vector_sums)
    return (input_grads, rate_grad, input_grad, vector_grads.reshape(1, 3, WIDTH))


def solution(mesh):
    in_specs = (
        P("section", None, "seq", "chan"),
        P(None, "seq", "chan"),
        P("section", "chan", None, None),
        P("section", "chan", None, None),
        P("section", "chan"),
        P("section", "chan"),
        P("section", "chan"),
        P("section", "chan"),
        P(),
    )
    out_specs = (
        P("section", None, "seq", "chan"),
        P("section", "chan", None, None),
        P("section", "chan", None, None),
        P("section", None, "chan"),
    )
    return jax.shard_map(
        on_device, mesh=mesh, in_specs=in_specs, out_specs=out_specs, check_vma=False
    )
```

```python
import math

import jax
import jax.numpy as jnp
from jax import lax
from jax.experimental import pallas as pl
from jax.experimental.pallas import tpu as pltpu
from jax.sharding import PartitionSpec as P

F32 = jnp.float32
BF16 = jnp.bfloat16
NX, NZ, NY = 4, 8, 4
MICRO, ROWS, WIDTH = 4, 64, 1024
HEADS, HEAD = 4, 256
FULL = WIDTH * NY
GROUPS = 2
MG = MICRO // GROUPS
GR = MG * ROWS
MESH = pl.DeviceIdType.MESH
FAR_Z = (4, 3, 5, 2, 6, 1, 7)
FAR_4 = (2, 1, 3)


def dot(a, b):
    return jnp.dot(a, b, preferred_element_type=F32)


def dot_t(a, b):
    return lax.dot_general(a, b, (((1,), (1,)), ((), ())), preferred_element_type=F32)


def sublane(shape):
    return lax.broadcasted_iota(jnp.int32, shape, 0)


def lane(shape):
    return lax.broadcasted_iota(jnp.int32, shape, 1)


def log1p_of(v):
    series = v * (1.0 - v * (0.5 - v * (1.0 / 3.0 - v * (0.25 - v * 0.2))))
    return jnp.where(v < 0.03125, series, jnp.log(1.0 + v))


def log_of(a):
    return jnp.log(jnp.maximum(a, 1e-37))


def decay_of(tile):
    wide = tile.astype(F32)
    return jnp.where(wide < -80.0, 0.0, jnp.exp(wide))


def body(
    x_hbm, up_hbm, rw_hbm, iw_hbm, rb_hbm, ib_hbm, dp_hbm, gain_hbm, starts_hbm,
    igv, wgo, vec_ref,
    rb_ref, ib_ref, dp_ref, gain_ref, starts_ref,
    xv, upv, rwv, iwv, xp, nd, dec, drv, mi, rr, kk, cc, upp, sv, dg, gb, keep, invb, inv_t, fb,
    ea, eh, eba, ebq, pa_s, fzt, bzt, za, fzs, fzr, fxs, fxr, bzs, bzr, bxs, bxr, stin, qin, zpre, zsuf,
    s1, s1r, ca, s2, s2r, vacc, vzs, vzr, vxs, vxr,
    ndt, wgb, rx, rs1, rz, z0, t0, x0,
    loc_sem, s1_ss, s1_rs, s2_ss, s2_rs, fz_ss, fz_rs, fx_ss, fx_rs, bz_ss, bz_rs, bx_ss, bx_rs,
    up_ss, up_rs, vz_ss, vz_rs, vx_ss, vx_rs, rx_ss, rx_rs, rz_ss, rz_rs, az_ss, az_rs, ax_ss, ax_rs, gate,
    z0_ss, z0_rs, x0_ss, x0_rs, bx0_ss, bx0_rs, bz0_ss, bz0_rs,
):
    sec = lax.axis_index("section")
    seq = lax.axis_index("seq")
    chan = lax.axis_index("chan")
    x_at = seq // NZ
    z_at = seq % NZ

    def z_peer(d):
        return {"seq": x_at * NZ + (z_at + d) % NZ}

    def x_peer(d):
        return {"seq": ((x_at + d) % NX) * NZ + z_at}

    def y_peer(d):
        return {"chan": (chan + d) % NY}

    other_core = {"section": 1 - sec}

    def remote(src, dst, ss, rs, to):
        return pltpu.make_async_remote_copy(
            src_ref=src, dst_ref=dst, send_sem=ss, recv_sem=rs, device_id=to, device_id_type=MESH
        )

    loads = [
        pltpu.make_async_copy(x_hbm.at[0], xv, loc_sem.at[0]),
        pltpu.make_async_copy(starts_hbm, starts_ref, loc_sem.at[4]),
    ]
    w_loads = [
        pltpu.make_async_copy(gain_hbm, gain_ref, loc_sem.at[5]),
        pltpu.make_async_copy(dp_hbm, dp_ref, loc_sem.at[6]),
        pltpu.make_async_copy(rb_hbm, rb_ref, loc_sem.at[7]),
        pltpu.make_async_copy(ib_hbm, ib_ref, loc_sem.at[8]),
        pltpu.make_async_copy(rw_hbm.at[0], rwv, loc_sem.at[1]),
        pltpu.make_async_copy(iw_hbm.at[0], iwv, loc_sem.at[2]),
    ]
    up_load = pltpu.make_async_copy(up_hbm, upv, loc_sem.at[3])
    for c in loads + w_loads:
        c.start()

    @pl.when(sec == 1)
    def _():
        up_load.start()

    barrier = pltpu.get_barrier_semaphore()
    peers = [z_peer(d) for d in range(1, NZ)] + [x_peer(d) for d in range(1, NX)]
    peers += [y_peer(d) for d in range(1, NY)] + [other_core]
    for to in peers:
        pl.semaphore_signal(barrier, inc=1, device_id=to, device_id_type=MESH)

    r_i = sublane((ROWS, ROWS))
    t_i = lane((ROWS, ROWS))
    perm = jnp.where(t_i == (r_i % 8) * 8 + r_i // 8, 1.0, 0.0).astype(BF16)
    perm_back = jnp.where(r_i == (t_i % 8) * 8 + t_i // 8, 1.0, 0.0).astype(BF16)

    vacc[...] = jnp.zeros_like(vacc)
    ca[...] = jnp.zeros_like(ca)


    for c in loads:
        c.wait()
    lane_t = lane((8, 128))
    tile = jnp.zeros((8, 128), F32)
    for m in range(MICRO):
        x_m = dot(perm, xv[m])
        acc = jnp.zeros((ROWS, 128), F32)
        for k in range(HEADS):
            x_k = x_m[:, k * HEAD : (k + 1) * HEAD]
            xp[k, m * ROWS : (m + 1) * ROWS, :] = x_k
            sq = x_k * x_k
            acc = acc + (sq[:, :128] + sq[:, 128:])
        for j in range(8):
            col = jnp.sum(acc[j * 8 : j * 8 + 8], axis=1, keepdims=True)
            tile = jnp.where(lane_t == m * 8 + j, col, tile)
    s1[...] = tile
    pl.semaphore_wait(barrier, len(peers))
    s1_copies = [
        remote(s1, s1r.at[d - 1], s1_ss.at[d - 1], s1_rs.at[d - 1], y_peer(d)) for d in range(1, NY)
    ]
    for c in s1_copies:
        c.start()
    r_w = sublane((ROWS, HEAD))
    position = seq * ROWS + (r_w % 8) * 8 + r_w // 8
    for m in range(MICRO):
        reset = position == 0
        for d in range(3):
            reset = jnp.logical_or(reset, position == starts_ref[m, d])
        keep[m] = jnp.where(reset, 0.0, 1.0)
    for c in w_loads:
        c.wait()
    for c in s1_copies:
        c.wait_recv()
    inv_tile = lax.rsqrt((s1[...] + s1r[0] + s1r[1] + s1r[2]) / FULL + 1e-06)
    inv_t[...] = inv_tile
    for m in range(MICRO):
        for j in range(8):
            at = m * 8 + j
            invb[m, j * 8 : j * 8 + 8, :] = jnp.broadcast_to(inv_tile[:, at : at + 1], (8, HEAD))

    sub = sublane((8, HEAD))

    def scan_up(a, h):
        for sh in (1, 2, 4):
            ok = sub >= sh
            h = h + a * jnp.where(ok, pltpu.roll(h, sh, 0), 0.0)
            a = a * jnp.where(ok, pltpu.roll(a, sh, 0), 1.0)
        return a, h

    def scan_down(a, h):
        for sh in (1, 2, 4):
            ok = sub < 8 - sh
            h = h + a * jnp.where(ok, pltpu.roll(h, 8 - sh, 0), 0.0)
            a = a * jnp.where(ok, pltpu.roll(a, 8 - sh, 0), 1.0)
        return a, h

    def to_tile(ref, index, k, row):
        for half in range(2):
            ref[(*index, pl.ds(k * 2 + half, 1), slice(None))] = row[:, half * 128 : half * 128 + 128]

    def from_tile(ref, index, k):
        return jnp.concatenate(
            [ref[(*index, pl.ds(k * 2 + half, 1), slice(None))] for half in range(2)], axis=1
        )

    def head_lanes(k):
        return pl.ds(pl.multiple_of(k * HEAD, HEAD), HEAD)

    def forward_head(g, k):
        gain = gain_ref[:, head_lanes(k)]
        rb = rb_ref[:, head_lanes(k)]
        ib = ib_ref[:, head_lanes(k)]
        v = dp_ref[:, head_lanes(k)]
        rate = -8.0 * (jnp.maximum(-v, 0.0) + log1p_of(jnp.exp(-jnp.abs(v))))
        for m in range(g * MG, (g + 1) * MG):
            rows = slice(m * ROWS, (m + 1) * ROWS)
            nd[k, rows, :] = (xp[k, rows, :] * invb[m] * gain).astype(BF16)
        grow = slice(g * GR, (g + 1) * GR)
        n_g = nd[k, grow, :]
        pre_r = dot(n_g, rwv[k])
        pre_i = dot(n_g, iwv[k])
        for m in range(g * MG, (g + 1) * MG):
            rows = slice(m * ROWS, (m + 1) * ROWS)
            own = slice((m - g * MG) * ROWS, (m - g * MG + 1) * ROWS)
            rg = 0.5 * jnp.tanh(0.5 * (pre_r[own] + rb)) + 0.5
            ig = 0.5 * jnp.tanh(0.5 * (pre_i[own] + ib)) + 0.5
            nw = n_g[own].astype(F32)
            kept = keep[m]
            ld = rate * rg
            e = jnp.exp(ld)
            gap = e * e
            u = ld + ld
            series = -u * (1.0 + u * (0.5 + u * (1.0 / 6.0 + u * (1.0 / 24.0 + u * (1.0 / 120.0)))))
            em = jnp.where(u > -0.125, series, 1.0 - gap)
            em = jnp.maximum(em, 1e-06)
            rs = lax.rsqrt(em)
            mult = jnp.where(kept > 0.5, em * rs, 1.0)
            a = e * kept
            mig = mult * ig
            b = mig * nw
            dec[k, rows, :] = a
            drv[k, rows, :] = b
            mi[k, rows, :] = mig
            rr[k, rows, :] = kept * (ig * nw * gap * rs)
            kk[k, rows, :] = ld * (1.0 - rg)
            cc[k, rows, :] = b * (1.0 - ig)
            pa = a[:8]
            h = b[:8]
            for j in range(1, 8):
                a_j = a[j * 8 : j * 8 + 8]
                h = a_j * h + b[j * 8 : j * 8 + 8]
                pa = pa * a_j
            seg = slice(m * 8, m * 8 + 8)
            pa_s[k, seg, :] = pa
            a_in, h_in = scan_up(pa, h)
            ea[k, seg, :] = jnp.where(sub >= 1, pltpu.roll(a_in, 1, 0), 1.0)
            eh[k, seg, :] = jnp.where(sub >= 1, pltpu.roll(h_in, 1, 0), 0.0)
            to_tile(fzt, (m, 0), k, a_in[7:8])
            to_tile(fzt, (m, 1), k, h_in[7:8])

    def group(g):
        return pl.ds(g * MG, MG)

    def fz(g, d):
        return remote(
            fzs.at[group(g)], fzr.at[d - 1, group(g)], fz_ss.at[g, d - 1], fz_rs.at[g, d - 1], z_peer(d)
        )

    def fx(g, d):
        return remote(
            fxs.at[group(g)], fxr.at[d - 1, group(g)], fx_ss.at[g, d - 1], fx_rs.at[g, d - 1], x_peer(d)
        )

    def bz(g, d):
        return remote(
            bzs.at[group(g)], bzr.at[d - 1, group(g)], bz_ss.at[g, d - 1], bz_rs.at[g, d - 1], z_peer(d)
        )

    def bx(g, d):
        return remote(
            bxs.at[group(g)], bxr.at[d - 1, group(g)], bx_ss.at[g, d - 1], bx_rs.at[g, d - 1], x_peer(d)
        )

    def back_local(g):
        for m in range(g * MG, (g + 1) * MG):
            u_m = dot(perm, upv[m])
            for k in range(HEADS):
                upp[k, m * ROWS : (m + 1) * ROWS, :] = u_m[:, k * HEAD : (k + 1) * HEAD]

        for k in range(HEADS):
            for m in range(g * MG, (g + 1) * MG):
                q = jnp.zeros((8, HEAD), F32)
                for j in range(7, -1, -1):
                    at = slice(m * ROWS + j * 8, m * ROWS + j * 8 + 8)
                    q = dec[k, at, :] * (upp[k, at, :] + q)
                seg = slice(m * 8, m * 8 + 8)
                a_in, q_in = scan_down(pa_s[k, seg, :], q)
                eba[k, seg, :] = jnp.where(sub < 7, pltpu.roll(a_in, 7, 0), 1.0)
                ebq[k, seg, :] = jnp.where(sub < 7, pltpu.roll(q_in, 7, 0), 0.0)
                to_tile(bzt, (m,), k, q_in[0:1])
        for m in range(g * MG, (g + 1) * MG):
            bzs[m] = bzt[m].astype(BF16)
        for d in FAR_Z:
            bz(g, d).start()

    @pl.when(sec == 1)
    def _():
        up_load.wait()

    for g in range(GROUPS):
        for k in range(HEADS):
            forward_head(g, k)
        for m in range(g * MG, (g + 1) * MG):
            fzs[m, 0] = log_of(fzt[m, 0]).astype(BF16)
            fzs[m, 1] = fzt[m, 1].astype(BF16)
        for d in FAR_Z:
            fz(g, d).start()

        @pl.when(sec == 1)
        def _(g=g):
            back_local(g)

    def turn_k(k, carry):
        ndt[k] = nd[k].T
        return carry

    lax.fori_loop(0, HEADS, turn_k, 0)

    def forward_totals(g):
        for d in range(1, NZ):
            fz(g, d).wait_recv()
        for m in range(g * MG, (g + 1) * MG):
            a_own, h_own = fzt[m, 0], fzt[m, 1]
            a_pre, h_pre = jnp.ones((8, 128), F32), jnp.zeros((8, 128), F32)
            a_suf, h_suf = a_pre, h_pre
            for d in range(1, NZ):
                ok = z_at >= d
                h_pre = h_pre + a_pre * jnp.where(ok, fzr[d - 1, m, 1].astype(F32), 0.0)
                a_d = decay_of(fzr[d - 1, m, 0])
                za[d - 1, m] = a_d
                a_pre = a_pre * jnp.where(ok, a_d, 1.0)
            for d in range(1, NZ):
                ok = z_at + d < NZ
                a_d = jnp.where(ok, za[NZ - d - 1, m], 1.0)
                h_suf = jnp.where(ok, fzr[NZ - d - 1, m, 1].astype(F32), 0.0) + a_d * h_suf
                a_suf = a_suf * a_d
            zpre[m, 0] = a_pre
            zpre[m, 1] = h_pre
            zsuf[m] = a_suf
            fxs[m, 0] = log_of(a_pre * a_own * a_suf).astype(BF16)
            fxs[m, 1] = (h_suf + a_suf * (h_own + a_own * h_pre)).astype(BF16)
        for d in FAR_4:
            fx(g, d).start()

    def up_copy(g):
        return remote(igv.at[group(g)], upv.at[group(g)], up_ss.at[g], up_rs.at[g], other_core)

    def backward_totals(g):
        for d in range(1, NZ):
            bz(g, d).wait_recv()
        for m in range(g * MG, (g + 1) * MG):
            a_run, q_run = jnp.ones((8, 128), F32), jnp.zeros((8, 128), F32)
            for d in range(1, NZ):
                ok = z_at + d < NZ
                q_run = q_run + a_run * jnp.where(ok, bzr[NZ - d - 1, m].astype(F32), 0.0)
                a_run = a_run * jnp.where(ok, za[NZ - d - 1, m], 1.0)
            qin[m] = q_run
            total = bzt[m] + fzt[m, 0] * q_run
            for d in range(1, NZ):
                ok = z_at >= d
                total = jnp.where(ok, bzr[d - 1, m].astype(F32) + za[d - 1, m] * total, total)
            bxs[m] = total.astype(BF16)
        for d in FAR_4:
            bx(g, d).start()

    def state_carry(g):
        for d in range(1, NX):
            fx(g, d).wait_recv()
        for m in range(g * MG, (g + 1) * MG):
            a_run, h_run = jnp.ones((8, 128), F32), jnp.zeros((8, 128), F32)
            for d in range(1, NX):
                ok = x_at >= d
                h_run = h_run + a_run * jnp.where(ok, fxr[d - 1, m, 1].astype(F32), 0.0)
                a_run = a_run * jnp.where(ok, decay_of(fxr[d - 1, m, 0]), 1.0)
            stin[m] = zpre[m, 1] + zpre[m, 0] * h_run

    for g in range(GROUPS):
        forward_totals(g)

        @pl.when(sec == 1)
        def _(g=g):
            backward_totals(g)

    @pl.when(sec == 0)
    def _():
        for g in range(GROUPS):
            state_carry(g)
        for g in range(GROUPS):
            up_copy(g).wait_recv()
            back_local(g)

    @pl.when(sec == 0)
    def _():
        for g in range(GROUPS):
            backward_totals(g)

    def s2_copy(g, d):
        return remote(s2.at[g], s2r.at[g, d - 1], s2_ss.at[g, d - 1], s2_rs.at[g, d - 1], y_peer(d))

    def q_carry(g):
        for d in range(1, NX):
            bx(g, d).wait_recv()
        for m in range(g * MG, (g + 1) * MG):
            a_run, q_run = jnp.ones((8, 128), F32), jnp.zeros((8, 128), F32)
            for d in range(1, NX):
                ok = x_at + d < NX
                q_run = q_run + a_run * jnp.where(ok, bxr[NX - d - 1, m].astype(F32), 0.0)
                a_run = a_run * jnp.where(ok, decay_of(fxr[NX - d - 1, m, 0]), 1.0)
            qin[m] = qin[m] + zsuf[m] * q_run

    def grad_head(k, low, high):
        gain = gain_ref[:, head_lanes(k)]
        v0 = vacc[0, k]
        v1 = vacc[1, k]
        v2 = vacc[2, k]
        for m in range(low, high):
            seg = slice(m * 8, m * 8 + 8)
            prev = eh[k, seg, :] + ea[k, seg, :] * from_tile(stin, (m,), k)
            q = ebq[k, seg, :] + eba[k, seg, :] * from_tile(qin, (m,), k)
            terms = []
            for j in range(8):
                at = slice(m * ROWS + j * 8, m * ROWS + j * 8 + 8)
                t = dec[k, at, :] * prev
                terms.append((t - rr[k, at, :]) * kk[k, at, :])
                prev = t + drv[k, at, :]
            rate_rows, input_rows = [None] * 8, [None] * 8
            for j in range(7, -1, -1):
                at = slice(m * ROWS + j * 8, m * ROWS + j * 8 + 8)
                sg = upp[k, at, :] + q
                q = dec[k, at, :] * sg
                rate_rows[j] = sg * terms[j]
                input_rows[j] = sg * cc[k, at, :]
                dg[k, at, :] = sg * mi[k, at, :]
            gr = jnp.concatenate(rate_rows, axis=0).astype(BF16)
            gi = jnp.concatenate(input_rows, axis=0).astype(BF16)
            rows = slice(m * ROWS, (m + 1) * ROWS)
            gb[k, rows, :HEAD] = gr
            gb[k, rows, HEAD:] = gi
            v0 = v0 + jnp.sum(gr.astype(F32).reshape(8, 8, HEAD), axis=0)
            v1 = v1 + jnp.sum(gi.astype(F32).reshape(8, 8, HEAD), axis=0)
        grow = slice(low * ROWS, high * ROWS)
        bp = dot_t(gb[k, grow, :HEAD], rwv[k]) + dot_t(gb[k, grow, HEAD:], iwv[k])
        for m in range(low, high):
            rows = slice(m * ROWS, (m + 1) * ROWS)
            own = slice((m - low) * ROWS, (m - low + 1) * ROWS)
            gn = dg[k, rows, :] + bp[own]
            w = gn * xp[k, rows, :]
            v2 = v2 + jnp.sum((w * invb[m]).reshape(8, 8, HEAD), axis=0)
            wg = w * gain
            ca[m] += wg[:, :128] + wg[:, 128:]
            sv[k, rows, :] = upp[k, rows, :] + gn * gain * invb[m]
        vacc[0, k] = v0
        vacc[1, k] = v1
        vacc[2, k] = v2

    def cross_sums(g):
        tile = jnp.zeros((8, 128), F32)
        for m in range(g * MG, (g + 1) * MG):
            for j in range(8):
                col = jnp.sum(ca[m, j * 8 : j * 8 + 8, :], axis=1, keepdims=True)
                tile = jnp.where(lane_t == m * 8 + j, col, tile)
        s2[g] = tile
        for d in FAR_4:
            s2_copy(g, d).start()

    def rx_copy(k, d):
        return remote(
            wgb.at[k, (x_at + d) % NX], rx.at[k, d - 1], rx_ss.at[k, d - 1], rx_rs.at[k, d - 1], x_peer(d)
        )

    def z0_copy(d):
        return remote(
            wgb.at[0, :, (z_at + d) % NZ], z0.at[d - 1], z0_ss.at[d - 1], z0_rs.at[d - 1], z_peer(d)
        )

    def x0_copy(d):
        return remote(t0.at[(x_at + d) % NX], x0.at[d - 1], x0_ss.at[d - 1], x0_rs.at[d - 1], x_peer(d))

    def bx0_copy(d, arrival=False):
        ref = wgo.at[(x_at + NX - d) % NX if arrival else x_at, z_at, 0]
        return remote(ref, ref, bx0_ss.at[d - 1], bx0_rs.at[d - 1], x_peer(d))

    def bz0_copy(d, arrival=False):
        ref = wgo.at[:, (z_at + NZ - d) % NZ if arrival else z_at, 0]
        return remote(ref, ref, bz0_ss.at[d - 1], bz0_rs.at[d - 1], z_peer(d))

    def head0_z():
        for d in range(1, NZ):
            z0_copy(d).wait_recv()
        total = wgb[0, :, z_at].astype(F32)
        for d in range(1, NZ):
            total = total + z0[d - 1].astype(F32)
        t0[...] = total.astype(BF16)
        for d in FAR_4:
            x0_copy(d).start()

    def head0_x():
        for d in range(1, NX):
            x0_copy(d).wait_recv()
        total = t0[x_at].astype(F32)
        for d in range(1, NX):
            total = total + x0[d - 1].astype(F32)
        wgo[x_at, z_at, 0] = total.astype(BF16)
        for d in FAR_4:
            bx0_copy(d).start()

    def head0_spread():
        for d in range(1, NX):
            bx0_copy(d, True).wait_recv()
        for d in FAR_Z:
            bz0_copy(d).start()

    def weight_head(k):
        w_k = dot(ndt[k], gb[k]).astype(BF16)
        for c in range(NX):
            for z in range(NZ):
                top = c * ROWS + (z // 2) * 16
                wgb[k, c, z] = w_k[top : top + 16, (z % 2) * HEAD : (z % 2) * HEAD + HEAD]
        if k == 0:
            for d in FAR_Z:
                z0_copy(d).start()
        else:
            for d in FAR_4:
                rx_copy(k, d).start()

    def rz_copy(k, d):
        return remote(
            rs1.at[k, (z_at + d) % NZ], rz.at[k, d - 1], rz_ss.at[k, d - 1], rz_rs.at[k, d - 1], z_peer(d)
        )

    def piece(x, z, p):
        return wgo.at[x, z, pl.ds(1, 2) if p == 0 else pl.ds(3, 1)]

    def from_z(d):
        return (z_at + NZ - d) % NZ

    def az_copy(p, d, arrival=False):
        ref = piece(x_at, from_z(d) if arrival else z_at, p)
        return remote(ref, ref, az_ss.at[p, d - 1], az_rs.at[p, d - 1], z_peer(d))

    def ax_copy(p, e, d, arrival=False):
        ref = piece((x_at + NX - e) % NX if arrival else x_at, from_z(d), p)
        return remote(ref, ref, ax_ss.at[p, e - 1, d], ax_rs.at[p, e - 1, d], x_peer(e))

    def spread(p, d):
        if d:
            az_copy(p, d, True).wait_recv()
        for e in FAR_4:
            ax_copy(p, e, d).start()

    def own_head(k):
        for d in range(1, NX):
            rx_copy(k, d).wait_recv()
        total = wgb[k, x_at].astype(F32)
        for d in range(1, NX):
            total = total + rx[k, d - 1].astype(F32)
        rs1[k] = total.astype(BF16)
        for d in FAR_Z:
            rz_copy(k, d).start()

    def vz_copy(d):
        return remote(vzs, vzr.at[d - 1], vz_ss.at[d - 1], vz_rs.at[d - 1], z_peer(d))

    def vx_copy(d):
        return remote(vxs, vxr.at[d - 1], vx_ss.at[d - 1], vx_rs.at[d - 1], x_peer(d))

    def vector_sums():
        for i in range(3):
            for k in range(HEADS):
                to_tile(vzs, (i,), k, jnp.sum(vacc[i, k], axis=0, keepdims=True))
        for d in FAR_Z:
            vz_copy(d).start()

    def finish_inputs(g):
        for d in range(1, NY):
            s2_copy(g, d).wait_recv()
        cross = s2[g] + s2r[g, 0] + s2r[g, 1] + s2r[g, 2]
        inv = inv_t[...]
        factor = cross * (inv * inv * inv) * (1.0 / FULL)
        for m in range(g * MG, (g + 1) * MG):
            for j in range(8):
                at = m * 8 + j
                fb[m, j * 8 : j * 8 + 8, :] = jnp.broadcast_to(factor[:, at : at + 1], (8, HEAD))
            rows = slice(m * ROWS, (m + 1) * ROWS)
            for k in range(HEADS):
                o = (sv[k, rows, :] - xp[k, rows, :] * fb[m]).astype(BF16)
                igv[m, :, k * HEAD : (k + 1) * HEAD] = dot(perm_back, o).astype(BF16)

    def gate_open():
        @pl.when(sec == 0)
        def _():
            pl.semaphore_signal(gate, inc=1, device_id=other_core, device_id_type=MESH)

    @pl.when(sec == 1)
    def _():
        for g in range(GROUPS):
            state_carry(g)
            q_carry(g)
            for k in range(HEADS):
                grad_head(k, g * MG, (g + 1) * MG)
            cross_sums(g)
        for k in range(HEADS):
            weight_head(k)

    @pl.when(sec == 0)
    def _():
        for g in range(GROUPS):
            q_carry(g)
        for k in range(HEADS):
            grad_head(k, 0, MICRO)
            weight_head(k)
        for g in range(GROUPS):
            cross_sums(g)

    vector_sums()

    @pl.when(sec == 1)
    def _():
        for g in range(GROUPS):
            finish_inputs(g)
            up_copy(g).start()

    own_head(1)
    gate_open()
    own_head(2)
    head0_z()
    own_head(3)

    @pl.when(sec == 0)
    def _():
        for g in range(GROUPS):
            finish_inputs(g)

    head0_x()

    for d in range(1, NZ):
        vz_copy(d).wait_recv()
    v_sum = vzs[...]
    for d in range(1, NZ):
        v_sum = v_sum + vzr[d - 1]
    vxs[...] = v_sum
    for d in FAR_4:
        vx_copy(d).start()

    for k in range(1, HEADS):
        for d in range(1, NZ):
            rz_copy(k, d).wait_recv()
        total = rs1[k, z_at].astype(F32)
        for d in range(1, NZ):
            total = total + rz[k, d - 1].astype(F32)
        wgo[x_at, z_at, k] = total.astype(BF16)
        if k > 1:
            for d in FAR_Z:
                az_copy(k - 2, d).start()
    head0_spread()

    @pl.when(sec == 1)
    def _():
        pl.semaphore_wait(gate, 1)

    for p in range(2):
        spread(p, 0)
    for near in ((1, 7), (2, 6), (3, 5)):
        for p in range(2):
            for d in near:
                spread(p, d)

    for p in range(2):
        spread(p, 4)

    for d in range(1, NX):
        vx_copy(d).wait_recv()
    v_sum = vxs[...]
    for d in range(1, NX):
        v_sum = v_sum + vxr[d - 1]
    vec_ref[...] = v_sum

    for d in range(1, NZ):
        bz0_copy(d, True).wait_recv()
    for p in range(2):
        for d in range(NZ):
            for e in range(1, NX):
                ax_copy(p, e, d, True).wait_recv()

    for c in s1_copies:
        c.wait_send()
    for g in range(GROUPS):
        for d in range(1, NZ):
            fz(g, d).wait_send()
            bz(g, d).wait_send()
        for d in range(1, NX):
            fx(g, d).wait_send()
            bx(g, d).wait_send()
        for d in range(1, NY):
            s2_copy(g, d).wait_send()

    @pl.when(sec == 1)
    def _():
        for g in range(GROUPS):
            up_copy(g).wait_send()

    for d in range(1, NZ):
        vz_copy(d).wait_send()
    for d in range(1, NX):
        vx_copy(d).wait_send()
    for d in range(1, NX):
        x0_copy(d).wait_send()
        bx0_copy(d).wait_send()
    for d in range(1, NZ):
        z0_copy(d).wait_send()
        bz0_copy(d).wait_send()
    for k in range(1, HEADS):
        for d in range(1, NX):
            rx_copy(k, d).wait_send()
        for d in range(1, NZ):
            rz_copy(k, d).wait_send()
    for p in range(2):
        for d in range(1, NZ):
            az_copy(p, d).wait_send()
        for d in range(NZ):
            for e in range(1, NX):
                ax_copy(p, e, d).wait_send()


def hand_out(ig_ref, w_ref, v_ref, ig_out, rate_out, input_out, v_out, staged, v_staged, sem):
    scale = 1.0 / math.sqrt(MICRO * ROWS * NX * NZ)
    copies = [pltpu.make_async_copy(ig_ref, ig_out.at[0], sem.at[0])]
    copies[0].start()
    v_staged[...] = v_ref[...] * scale
    copies.append(pltpu.make_async_copy(v_staged, v_out, sem.at[1]))
    copies[1].start()
    for k in range(HEADS):
        for c in range(NX):
            for z in range(NZ):
                top = c * ROWS + (z // 2) * 16
                staged[z % 2, k, top : top + 16, :] = w_ref[c, z, k].astype(F32) * scale
        for half, out in enumerate((rate_out, input_out)):
            copies.append(pltpu.make_async_copy(staged.at[half, k], out.at[0, k], sem.at[2 + 2 * k + half]))
            copies[-1].start()
    for c in copies:
        c.wait()


def on_device(*arguments):
    tokens = MICRO * ROWS
    wide = pltpu.VMEM((HEADS, tokens, HEAD), F32)
    seg = pltpu.VMEM((HEADS, MICRO * 8, HEAD), F32)
    dma = pltpu.SemaphoreType.DMA

    def tiles(*lead, dtype=F32):
        return pltpu.VMEM((*lead, 8, 128), dtype)

    row = pltpu.VMEM((1, WIDTH), F32)
    scratch = [
        row, row, row, row, pltpu.SMEM((MICRO, 3), jnp.int32),
        pltpu.VMEM((MICRO, ROWS, WIDTH), BF16),
        pltpu.VMEM((MICRO, ROWS, WIDTH), BF16),
        pltpu.VMEM((HEADS, HEAD, HEAD), BF16),
        pltpu.VMEM((HEADS, HEAD, HEAD), BF16),
        wide,
        pltpu.VMEM((HEADS, tokens, HEAD), BF16),
        wide, wide, wide, wide, wide, wide,
        wide, wide, wide,
        pltpu.VMEM((HEADS, tokens, 2 * HEAD), BF16),
        pltpu.VMEM((MICRO, ROWS, HEAD), F32),
        pltpu.VMEM((MICRO, ROWS, HEAD), F32),
        tiles(),
        pltpu.VMEM((MICRO, ROWS, HEAD), F32),
        seg, seg, seg, seg, seg,
        tiles(MICRO, 2), tiles(MICRO), tiles(NZ - 1, MICRO),
        tiles(MICRO, 2, dtype=BF16), tiles(NZ - 1, MICRO, 2, dtype=BF16),
        tiles(MICRO, 2, dtype=BF16), tiles(NX - 1, MICRO, 2, dtype=BF16),
        tiles(MICRO, dtype=BF16), tiles(NZ - 1, MICRO, dtype=BF16),
        tiles(MICRO, dtype=BF16), tiles(NX - 1, MICRO, dtype=BF16),
        tiles(MICRO), tiles(MICRO), tiles(MICRO, 2), tiles(MICRO),
        tiles(), tiles(NY - 1),
        pltpu.VMEM((MICRO, ROWS, 128), F32),
        tiles(GROUPS), tiles(GROUPS, NY - 1),
        pltpu.VMEM((3, HEADS, 8, HEAD), F32),
        tiles(3), tiles(NZ - 1, 3), tiles(3), tiles(NX - 1, 3),
        pltpu.VMEM((HEADS, HEAD, tokens), BF16),
        pltpu.VMEM((HEADS, NX, NZ, 16, HEAD), BF16),
        pltpu.VMEM((HEADS, NX - 1, NZ, 16, HEAD), BF16),
        pltpu.VMEM((HEADS, NZ, 16, HEAD), BF16),
        pltpu.VMEM((HEADS, NZ - 1, 16, HEAD), BF16),
        pltpu.VMEM((NZ - 1, NX, 16, HEAD), BF16),
        pltpu.VMEM((NX, 16, HEAD), BF16),
        pltpu.VMEM((NX - 1, 16, HEAD), BF16),
        dma((9,)),
    ]
    scratch += [dma((NY - 1,))] * 2 + [dma((GROUPS, NY - 1))] * 2
    scratch += ([dma((GROUPS, NZ - 1))] * 2 + [dma((GROUPS, NX - 1))] * 2) * 2
    scratch += [dma((GROUPS,))] * 2
    scratch += [dma((NZ - 1,))] * 2 + [dma((NX - 1,))] * 2
    scratch += [dma((HEADS, NX - 1))] * 2 + [dma((HEADS, NZ - 1))] * 2 + [dma((2, NZ - 1))] * 2
    scratch += [dma((2, NX - 1, NZ))] * 2 + [pltpu.SemaphoreType.REGULAR]
    scratch += [dma((NZ - 1,))] * 2 + [dma((NX - 1,))] * 4 + [dma((NZ - 1,))] * 2

    hbm = pl.BlockSpec(memory_space=pltpu.HBM)
    vmem = pl.BlockSpec(memory_space=pltpu.VMEM)
    input_grads, weight_sums, vector_sums = pl.pallas_call(
        body,
        out_shape=(
            jax.ShapeDtypeStruct((MICRO, ROWS, WIDTH), BF16),
            jax.ShapeDtypeStruct((NX, NZ, HEADS, 16, HEAD), BF16),
            jax.ShapeDtypeStruct((3, 8, 128), F32),
        ),
        in_specs=[hbm] * 9,
        out_specs=(vmem, vmem, vmem),
        scratch_shapes=scratch,
        compiler_params=pltpu.CompilerParams(
            collective_id=0, has_side_effects=True, vmem_limit_bytes=48 << 20
        ),
        name="rglru_backward",
    )(*(pltpu.with_memory_space_constraint(v, pltpu.HBM) for v in arguments))
    square = jax.ShapeDtypeStruct((1, HEADS, HEAD, HEAD), F32)
    input_grads, rate_grad, input_grad, vector_grads = pl.pallas_call(
        hand_out,
        out_shape=(
            jax.ShapeDtypeStruct((1, MICRO, ROWS, WIDTH), BF16), square, square,
            jax.ShapeDtypeStruct((3, 8, 128), F32),
        ),
        in_specs=[vmem] * 3,
        out_specs=(hbm, hbm, hbm, hbm),
        scratch_shapes=[
            pltpu.VMEM((2, HEADS, HEAD, HEAD), F32), pltpu.VMEM((3, 8, 128), F32), dma((2 + 2 * HEADS,)),
        ],
        compiler_params=pltpu.CompilerParams(vmem_limit_bytes=8 << 20),
        name="hand_out",
    )(input_grads, weight_sums, vector_sums)
    return (input_grads, rate_grad, input_grad, vector_grads.reshape(1, 3, WIDTH))


def solution(mesh):
    in_specs = (
        P("section", None, "seq", "chan"),
        P(None, "seq", "chan"),
        P("section", "chan", None, None),
        P("section", "chan", None, None),
        P("section", "chan"),
        P("section", "chan"),
        P("section", "chan"),
        P("section", "chan"),
        P(),
    )
    out_specs = (
        P("section", None, "seq", "chan"),
        P("section", "chan", None, None),
        P("section", "chan", None, None),
        P("section", None, "chan"),
    )
    return jax.shard_map(
        on_device, mesh=mesh, in_specs=in_specs, out_specs=out_specs, check_vma=False
    )
```

```python
import math

import jax
import jax.numpy as jnp
from jax import lax
from jax.experimental import pallas as pl
from jax.experimental.pallas import tpu as pltpu
from jax.sharding import PartitionSpec as P

F32 = jnp.float32
BF16 = jnp.bfloat16
NX, NZ, NY = 4, 8, 4
MICRO, ROWS, WIDTH = 4, 64, 1024
HEADS, HEAD = 4, 256
FULL = WIDTH * NY
GROUPS = 2
MG = MICRO // GROUPS
GR = MG * ROWS
MESH = pl.DeviceIdType.MESH
FAR_Z = (4, 3, 5, 2, 6, 1, 7)
FAR_4 = (2, 1, 3)


def dot(a, b):
    return jnp.dot(a, b, preferred_element_type=F32)


def dot_t(a, b):
    return lax.dot_general(a, b, (((1,), (1,)), ((), ())), preferred_element_type=F32)


def sublane(shape):
    return lax.broadcasted_iota(jnp.int32, shape, 0)


def lane(shape):
    return lax.broadcasted_iota(jnp.int32, shape, 1)


def log1p_of(v):
    series = v * (1.0 - v * (0.5 - v * (1.0 / 3.0 - v * (0.25 - v * 0.2))))
    return jnp.where(v < 0.03125, series, jnp.log(1.0 + v))


def log_of(a):
    return jnp.log(jnp.maximum(a, 1e-37))


def decay_of(tile):
    wide = tile.astype(F32)
    return jnp.where(wide < -80.0, 0.0, jnp.exp(wide))


def body(
    x_hbm, up_hbm, rw_hbm, iw_hbm, rb_hbm, ib_hbm, dp_hbm, gain_hbm, starts_hbm,
    igv, wgo, vec_ref,
    rb_ref, ib_ref, dp_ref, gain_ref, starts_ref,
    xv, upv, rwv, iwv, xp, nd, dec, drv, mi, rr, kk, cc, upp, sv, dg, gb, keep, invb, inv_t, fb,
    ea, eh, eba, ebq, pa_s, fzt, bzt, za, fzs, fzr, fxs, fxr, bzs, bzr, bxs, bxr, stin, qin, zpre, zsuf,
    s1, s1r, ca, s2, s2r, vacc, vzs, vzr, vxs, vxr,
    ndt, wgb, rx, rs1, rz, z0, t0, x0,
    loc_sem, s1_ss, s1_rs, s2_ss, s2_rs, fz_ss, fz_rs, fx_ss, fx_rs, bz_ss, bz_rs, bx_ss, bx_rs,
    up_ss, up_rs, vz_ss, vz_rs, vx_ss, vx_rs, rx_ss, rx_rs, rz_ss, rz_rs, az_ss, az_rs, ax_ss, ax_rs, gate,
    z0_ss, z0_rs, x0_ss, x0_rs, bx0_ss, bx0_rs, bz0_ss, bz0_rs,
):
    sec = lax.axis_index("section")
    seq = lax.axis_index("seq")
    chan = lax.axis_index("chan")
    x_at = seq // NZ
    z_at = seq % NZ

    def z_peer(d):
        return {"seq": x_at * NZ + (z_at + d) % NZ}

    def x_peer(d):
        return {"seq": ((x_at + d) % NX) * NZ + z_at}

    def y_peer(d):
        return {"chan": (chan + d) % NY}

    other_core = {"section": 1 - sec}

    def remote(src, dst, ss, rs, to):
        return pltpu.make_async_remote_copy(
            src_ref=src, dst_ref=dst, send_sem=ss, recv_sem=rs, device_id=to, device_id_type=MESH
        )

    loads = [
        pltpu.make_async_copy(x_hbm.at[0], xv, loc_sem.at[0]),
        pltpu.make_async_copy(starts_hbm, starts_ref, loc_sem.at[4]),
    ]
    w_loads = [
        pltpu.make_async_copy(gain_hbm, gain_ref, loc_sem.at[5]),
        pltpu.make_async_copy(dp_hbm, dp_ref, loc_sem.at[6]),
        pltpu.make_async_copy(rb_hbm, rb_ref, loc_sem.at[7]),
        pltpu.make_async_copy(ib_hbm, ib_ref, loc_sem.at[8]),
        pltpu.make_async_copy(rw_hbm.at[0], rwv, loc_sem.at[1]),
        pltpu.make_async_copy(iw_hbm.at[0], iwv, loc_sem.at[2]),
    ]
    up_load = pltpu.make_async_copy(up_hbm, upv, loc_sem.at[3])
    for c in loads + w_loads:
        c.start()

    @pl.when(sec == 1)
    def _():
        up_load.start()

    barrier = pltpu.get_barrier_semaphore()
    peers = [z_peer(d) for d in range(1, NZ)] + [x_peer(d) for d in range(1, NX)]
    peers += [y_peer(d) for d in range(1, NY)] + [other_core]
    for to in peers:
        pl.semaphore_signal(barrier, inc=1, device_id=to, device_id_type=MESH)

    r_i = sublane((ROWS, ROWS))
    t_i = lane((ROWS, ROWS))
    perm = jnp.where(t_i == (r_i % 8) * 8 + r_i // 8, 1.0, 0.0).astype(BF16)
    perm_back = jnp.where(r_i == (t_i % 8) * 8 + t_i // 8, 1.0, 0.0).astype(BF16)

    vacc[...] = jnp.zeros_like(vacc)
    ca[...] = jnp.zeros_like(ca)


    for c in loads:
        c.wait()
    lane_t = lane((8, 128))
    tile = jnp.zeros((8, 128), F32)
    for m in range(MICRO):
        x_m = dot(perm, xv[m])
        acc = jnp.zeros((ROWS, 128), F32)
        for k in range(HEADS):
            x_k = x_m[:, k * HEAD : (k + 1) * HEAD]
            xp[k, m * ROWS : (m + 1) * ROWS, :] = x_k
            sq = x_k * x_k
            acc = acc + (sq[:, :128] + sq[:, 128:])
        for j in range(8):
            col = jnp.sum(acc[j * 8 : j * 8 + 8], axis=1, keepdims=True)
            tile = jnp.where(lane_t == m * 8 + j, col, tile)
    s1[...] = tile
    pl.semaphore_wait(barrier, len(peers))
    s1_copies = [
        remote(s1, s1r.at[d - 1], s1_ss.at[d - 1], s1_rs.at[d - 1], y_peer(d)) for d in range(1, NY)
    ]
    for c in s1_copies:
        c.start()
    r_w = sublane((ROWS, HEAD))
    position = seq * ROWS + (r_w % 8) * 8 + r_w // 8
    for m in range(MICRO):
        reset = position == 0
        for d in range(3):
            reset = jnp.logical_or(reset, position == starts_ref[m, d])
        keep[m] = jnp.where(reset, 0.0, 1.0)
    for c in w_loads:
        c.wait()
    for c in s1_copies:
        c.wait_recv()
    inv_tile = lax.rsqrt((s1[...] + s1r[0] + s1r[1] + s1r[2]) / FULL + 1e-06)
    inv_t[...] = inv_tile
    for m in range(MICRO):
        for j in range(8):
            at = m * 8 + j
            invb[m, j * 8 : j * 8 + 8, :] = jnp.broadcast_to(inv_tile[:, at : at + 1], (8, HEAD))

    sub = sublane((8, HEAD))

    def scan_up(a, h):
        for sh in (1, 2, 4):
            ok = sub >= sh
            h = h + a * jnp.where(ok, pltpu.roll(h, sh, 0), 0.0)
            a = a * jnp.where(ok, pltpu.roll(a, sh, 0), 1.0)
        return a, h

    def scan_down(a, h):
        for sh in (1, 2, 4):
            ok = sub < 8 - sh
            h = h + a * jnp.where(ok, pltpu.roll(h, 8 - sh, 0), 0.0)
            a = a * jnp.where(ok, pltpu.roll(a, 8 - sh, 0), 1.0)
        return a, h

    def to_tile(ref, index, k, row):
        for half in range(2):
            ref[(*index, pl.ds(k * 2 + half, 1), slice(None))] = row[:, half * 128 : half * 128 + 128]

    def from_tile(ref, index, k):
        return jnp.concatenate(
            [ref[(*index, pl.ds(k * 2 + half, 1), slice(None))] for half in range(2)], axis=1
        )

    def head_lanes(k):
        return pl.ds(pl.multiple_of(k * HEAD, HEAD), HEAD)

    def forward_head(g, k):
        gain = gain_ref[:, head_lanes(k)]
        rb = rb_ref[:, head_lanes(k)]
        ib = ib_ref[:, head_lanes(k)]
        v = dp_ref[:, head_lanes(k)]
        rate = -8.0 * (jnp.maximum(-v, 0.0) + log1p_of(jnp.exp(-jnp.abs(v))))
        for m in range(g * MG, (g + 1) * MG):
            rows = slice(m * ROWS, (m + 1) * ROWS)
            nd[k, rows, :] = (xp[k, rows, :] * invb[m] * gain).astype(BF16)
        grow = slice(g * GR, (g + 1) * GR)
        n_g = nd[k, grow, :]
        pre_r = dot(n_g, rwv[k])
        pre_i = dot(n_g, iwv[k])
        for m in range(g * MG, (g + 1) * MG):
            rows = slice(m * ROWS, (m + 1) * ROWS)
            own = slice((m - g * MG) * ROWS, (m - g * MG + 1) * ROWS)
            rg = 0.5 * jnp.tanh(0.5 * (pre_r[own] + rb)) + 0.5
            ig = 0.5 * jnp.tanh(0.5 * (pre_i[own] + ib)) + 0.5
            nw = n_g[own].astype(F32)
            kept = keep[m]
            ld = rate * rg
            e = jnp.exp(ld)
            gap = e * e
            em = jnp.tanh(-ld) * (1.0 + gap)
            em = jnp.maximum(em, 1e-06)
            rs = lax.rsqrt(em)
            mult = jnp.where(kept > 0.5, em * rs, 1.0)
            a = e * kept
            mig = mult * ig
            b = mig * nw
            dec[k, rows, :] = a
            drv[k, rows, :] = b
            mi[k, rows, :] = mig
            rr[k, rows, :] = kept * (ig * nw * gap * rs)
            kk[k, rows, :] = ld * (1.0 - rg)
            cc[k, rows, :] = b * (1.0 - ig)
            pa = a[:8]
            h = b[:8]
            for j in range(1, 8):
                a_j = a[j * 8 : j * 8 + 8]
                h = a_j * h + b[j * 8 : j * 8 + 8]
                pa = pa * a_j
            seg = slice(m * 8, m * 8 + 8)
            pa_s[k, seg, :] = pa
            a_in, h_in = scan_up(pa, h)
            ea[k, seg, :] = jnp.where(sub >= 1, pltpu.roll(a_in, 1, 0), 1.0)
            eh[k, seg, :] = jnp.where(sub >= 1, pltpu.roll(h_in, 1, 0), 0.0)
            to_tile(fzt, (m, 0), k, a_in[7:8])
            to_tile(fzt, (m, 1), k, h_in[7:8])

    def group(g):
        return pl.ds(g * MG, MG)

    def fz(g, d):
        return remote(
            fzs.at[group(g)], fzr.at[d - 1, group(g)], fz_ss.at[g, d - 1], fz_rs.at[g, d - 1], z_peer(d)
        )

    def fx(g, d):
        return remote(
            fxs.at[group(g)], fxr.at[d - 1, group(g)], fx_ss.at[g, d - 1], fx_rs.at[g, d - 1], x_peer(d)
        )

    def bz(g, d):
        return remote(
            bzs.at[group(g)], bzr.at[d - 1, group(g)], bz_ss.at[g, d - 1], bz_rs.at[g, d - 1], z_peer(d)
        )

    def bx(g, d):
        return remote(
            bxs.at[group(g)], bxr.at[d - 1, group(g)], bx_ss.at[g, d - 1], bx_rs.at[g, d - 1], x_peer(d)
        )

    def back_local(g):
        for m in range(g * MG, (g + 1) * MG):
            u_m = dot(perm, upv[m])
            for k in range(HEADS):
                upp[k, m * ROWS : (m + 1) * ROWS, :] = u_m[:, k * HEAD : (k + 1) * HEAD]

        for k in range(HEADS):
            for m in range(g * MG, (g + 1) * MG):
                q = jnp.zeros((8, HEAD), F32)
                for j in range(7, -1, -1):
                    at = slice(m * ROWS + j * 8, m * ROWS + j * 8 + 8)
                    q = dec[k, at, :] * (upp[k, at, :] + q)
                seg = slice(m * 8, m * 8 + 8)
                a_in, q_in = scan_down(pa_s[k, seg, :], q)
                eba[k, seg, :] = jnp.where(sub < 7, pltpu.roll(a_in, 7, 0), 1.0)
                ebq[k, seg, :] = jnp.where(sub < 7, pltpu.roll(q_in, 7, 0), 0.0)
                to_tile(bzt, (m,), k, q_in[0:1])
        for m in range(g * MG, (g + 1) * MG):
            bzs[m] = bzt[m].astype(BF16)
        for d in FAR_Z:
            bz(g, d).start()

    @pl.when(sec == 1)
    def _():
        up_load.wait()

    for g in range(GROUPS):
        for k in range(HEADS):
            forward_head(g, k)
        for m in range(g * MG, (g + 1) * MG):
            fzs[m, 0] = log_of(fzt[m, 0]).astype(BF16)
            fzs[m, 1] = fzt[m, 1].astype(BF16)
        for d in FAR_Z:
            fz(g, d).start()

        @pl.when(sec == 1)
        def _(g=g):
            back_local(g)

    def turn_k(k, carry):
        ndt[k] = nd[k].T
        return carry

    lax.fori_loop(0, HEADS, turn_k, 0)

    def forward_totals(g):
        for d in range(1, NZ):
            fz(g, d).wait_recv()
        for m in range(g * MG, (g + 1) * MG):
            a_own, h_own = fzt[m, 0], fzt[m, 1]
            a_pre, h_pre = jnp.ones((8, 128), F32), jnp.zeros((8, 128), F32)
            a_suf, h_suf = a_pre, h_pre
            for d in range(1, NZ):
                ok = z_at >= d
                h_pre = h_pre + a_pre * jnp.where(ok, fzr[d - 1, m, 1].astype(F32), 0.0)
                a_d = decay_of(fzr[d - 1, m, 0])
                za[d - 1, m] = a_d
                a_pre = a_pre * jnp.where(ok, a_d, 1.0)
            for d in range(1, NZ):
                ok = z_at + d < NZ
                a_d = jnp.where(ok, za[NZ - d - 1, m], 1.0)
                h_suf = jnp.where(ok, fzr[NZ - d - 1, m, 1].astype(F32), 0.0) + a_d * h_suf
                a_suf = a_suf * a_d
            zpre[m, 0] = a_pre
            zpre[m, 1] = h_pre
            zsuf[m] = a_suf
            fxs[m, 0] = log_of(a_pre * a_own * a_suf).astype(BF16)
            fxs[m, 1] = (h_suf + a_suf * (h_own + a_own * h_pre)).astype(BF16)
        for d in FAR_4:
            fx(g, d).start()

    def up_copy(g):
        return remote(igv.at[group(g)], upv.at[group(g)], up_ss.at[g], up_rs.at[g], other_core)

    def backward_totals(g):
        for d in range(1, NZ):
            bz(g, d).wait_recv()
        for m in range(g * MG, (g + 1) * MG):
            a_run, q_run = jnp.ones((8, 128), F32), jnp.zeros((8, 128), F32)
            for d in range(1, NZ):
                ok = z_at + d < NZ
                q_run = q_run + a_run * jnp.where(ok, bzr[NZ - d - 1, m].astype(F32), 0.0)
                a_run = a_run * jnp.where(ok, za[NZ - d - 1, m], 1.0)
            qin[m] = q_run
            total = bzt[m] + fzt[m, 0] * q_run
            for d in range(1, NZ):
                ok = z_at >= d
                total = jnp.where(ok, bzr[d - 1, m].astype(F32) + za[d - 1, m] * total, total)
            bxs[m] = total.astype(BF16)
        for d in FAR_4:
            bx(g, d).start()

    def state_carry(g):
        for d in range(1, NX):
            fx(g, d).wait_recv()
        for m in range(g * MG, (g + 1) * MG):
            a_run, h_run = jnp.ones((8, 128), F32), jnp.zeros((8, 128), F32)
            for d in range(1, NX):
                ok = x_at >= d
                h_run = h_run + a_run * jnp.where(ok, fxr[d - 1, m, 1].astype(F32), 0.0)
                a_run = a_run * jnp.where(ok, decay_of(fxr[d - 1, m, 0]), 1.0)
            stin[m] = zpre[m, 1] + zpre[m, 0] * h_run

    for g in range(GROUPS):
        forward_totals(g)

        @pl.when(sec == 1)
        def _(g=g):
            backward_totals(g)

    @pl.when(sec == 0)
    def _():
        for g in range(GROUPS):
            state_carry(g)
        for g in range(GROUPS):
            up_copy(g).wait_recv()
            back_local(g)

    @pl.when(sec == 0)
    def _():
        for g in range(GROUPS):
            backward_totals(g)

    def s2_copy(g, d):
        return remote(s2.at[g], s2r.at[g, d - 1], s2_ss.at[g, d - 1], s2_rs.at[g, d - 1], y_peer(d))

    def q_carry(g):
        for d in range(1, NX):
            bx(g, d).wait_recv()
        for m in range(g * MG, (g + 1) * MG):
            a_run, q_run = jnp.ones((8, 128), F32), jnp.zeros((8, 128), F32)
            for d in range(1, NX):
                ok = x_at + d < NX
                q_run = q_run + a_run * jnp.where(ok, bxr[NX - d - 1, m].astype(F32), 0.0)
                a_run = a_run * jnp.where(ok, decay_of(fxr[NX - d - 1, m, 0]), 1.0)
            qin[m] = qin[m] + zsuf[m] * q_run

    def grad_head(k, low, high):
        gain = gain_ref[:, head_lanes(k)]
        v0 = vacc[0, k]
        v1 = vacc[1, k]
        v2 = vacc[2, k]
        for m in range(low, high):
            seg = slice(m * 8, m * 8 + 8)
            prev = eh[k, seg, :] + ea[k, seg, :] * from_tile(stin, (m,), k)
            q = ebq[k, seg, :] + eba[k, seg, :] * from_tile(qin, (m,), k)
            terms = []
            for j in range(8):
                at = slice(m * ROWS + j * 8, m * ROWS + j * 8 + 8)
                t = dec[k, at, :] * prev
                terms.append((t - rr[k, at, :]) * kk[k, at, :])
                prev = t + drv[k, at, :]
            rate_rows, input_rows = [None] * 8, [None] * 8
            for j in range(7, -1, -1):
                at = slice(m * ROWS + j * 8, m * ROWS + j * 8 + 8)
                sg = upp[k, at, :] + q
                q = dec[k, at, :] * sg
                rate_rows[j] = sg * terms[j]
                input_rows[j] = sg * cc[k, at, :]
                dg[k, at, :] = sg * mi[k, at, :]
            gr = jnp.concatenate(rate_rows, axis=0).astype(BF16)
            gi = jnp.concatenate(input_rows, axis=0).astype(BF16)
            rows = slice(m * ROWS, (m + 1) * ROWS)
            gb[k, rows, :HEAD] = gr
            gb[k, rows, HEAD:] = gi
            v0 = v0 + jnp.sum(gr.astype(F32).reshape(8, 8, HEAD), axis=0)
            v1 = v1 + jnp.sum(gi.astype(F32).reshape(8, 8, HEAD), axis=0)
        grow = slice(low * ROWS, high * ROWS)
        bp = dot_t(gb[k, grow, :HEAD], rwv[k]) + dot_t(gb[k, grow, HEAD:], iwv[k])
        for m in range(low, high):
            rows = slice(m * ROWS, (m + 1) * ROWS)
            own = slice((m - low) * ROWS, (m - low + 1) * ROWS)
            gn = dg[k, rows, :] + bp[own]
            w = gn * xp[k, rows, :]
            v2 = v2 + jnp.sum((w * invb[m]).reshape(8, 8, HEAD), axis=0)
            wg = w * gain
            ca[m] += wg[:, :128] + wg[:, 128:]
            sv[k, rows, :] = upp[k, rows, :] + gn * gain * invb[m]
        vacc[0, k] = v0
        vacc[1, k] = v1
        vacc[2, k] = v2

    def cross_sums(g):
        tile = jnp.zeros((8, 128), F32)
        for m in range(g * MG, (g + 1) * MG):
            for j in range(8):
                col = jnp.sum(ca[m, j * 8 : j * 8 + 8, :], axis=1, keepdims=True)
                tile = jnp.where(lane_t == m * 8 + j, col, tile)
        s2[g] = tile
        for d in FAR_4:
            s2_copy(g, d).start()

    def rx_copy(k, d):
        return remote(
            wgb.at[k, (x_at + d) % NX], rx.at[k, d - 1], rx_ss.at[k, d - 1], rx_rs.at[k, d - 1], x_peer(d)
        )

    def z0_copy(d):
        return remote(
            wgb.at[0, :, (z_at + d) % NZ], z0.at[d - 1], z0_ss.at[d - 1], z0_rs.at[d - 1], z_peer(d)
        )

    def x0_copy(d):
        return remote(t0.at[(x_at + d) % NX], x0.at[d - 1], x0_ss.at[d - 1], x0_rs.at[d - 1], x_peer(d))

    def bx0_copy(d, arrival=False):
        ref = wgo.at[(x_at + NX - d) % NX if arrival else x_at, z_at, 0]
        return remote(ref, ref, bx0_ss.at[d - 1], bx0_rs.at[d - 1], x_peer(d))

    def bz0_copy(d, arrival=False):
        ref = wgo.at[:, (z_at + NZ - d) % NZ if arrival else z_at, 0]
        return remote(ref, ref, bz0_ss.at[d - 1], bz0_rs.at[d - 1], z_peer(d))

    def head0_z():
        for d in range(1, NZ):
            z0_copy(d).wait_recv()
        total = wgb[0, :, z_at].astype(F32)
        for d in range(1, NZ):
            total = total + z0[d - 1].astype(F32)
        t0[...] = total.astype(BF16)
        for d in FAR_4:
            x0_copy(d).start()

    def head0_x():
        for d in range(1, NX):
            x0_copy(d).wait_recv()
        total = t0[x_at].astype(F32)
        for d in range(1, NX):
            total = total + x0[d - 1].astype(F32)
        wgo[x_at, z_at, 0] = total.astype(BF16)
        for d in FAR_4:
            bx0_copy(d).start()

    def head0_spread():
        for d in range(1, NX):
            bx0_copy(d, True).wait_recv()
        for d in FAR_Z:
            bz0_copy(d).start()

    def weight_head(k):
        w_k = dot(ndt[k], gb[k]).astype(BF16)
        for c in range(NX):
            for z in range(NZ):
                top = c * ROWS + (z // 2) * 16
                wgb[k, c, z] = w_k[top : top + 16, (z % 2) * HEAD : (z % 2) * HEAD + HEAD]
        if k == 0:
            for d in FAR_Z:
                z0_copy(d).start()
        else:
            for d in FAR_4:
                rx_copy(k, d).start()

    def rz_copy(k, d):
        return remote(
            rs1.at[k, (z_at + d) % NZ], rz.at[k, d - 1], rz_ss.at[k, d - 1], rz_rs.at[k, d - 1], z_peer(d)
        )

    def piece(x, z, p):
        return wgo.at[x, z, pl.ds(1, 2) if p == 0 else pl.ds(3, 1)]

    def from_z(d):
        return (z_at + NZ - d) % NZ

    def az_copy(p, d, arrival=False):
        ref = piece(x_at, from_z(d) if arrival else z_at, p)
        return remote(ref, ref, az_ss.at[p, d - 1], az_rs.at[p, d - 1], z_peer(d))

    def ax_copy(p, e, d, arrival=False):
        ref = piece((x_at + NX - e) % NX if arrival else x_at, from_z(d), p)
        return remote(ref, ref, ax_ss.at[p, e - 1, d], ax_rs.at[p, e - 1, d], x_peer(e))

    def spread(p, d):
        if d:
            az_copy(p, d, True).wait_recv()
        for e in FAR_4:
            ax_copy(p, e, d).start()

    def own_head(k):
        for d in range(1, NX):
            rx_copy(k, d).wait_recv()
        total = wgb[k, x_at].astype(F32)
        for d in range(1, NX):
            total = total + rx[k, d - 1].astype(F32)
        rs1[k] = total.astype(BF16)
        for d in FAR_Z:
            rz_copy(k, d).start()

    def vz_copy(d):
        return remote(vzs, vzr.at[d - 1], vz_ss.at[d - 1], vz_rs.at[d - 1], z_peer(d))

    def vx_copy(d):
        return remote(vxs, vxr.at[d - 1], vx_ss.at[d - 1], vx_rs.at[d - 1], x_peer(d))

    def vector_sums():
        for i in range(3):
            for k in range(HEADS):
                to_tile(vzs, (i,), k, jnp.sum(vacc[i, k], axis=0, keepdims=True))
        for d in FAR_Z:
            vz_copy(d).start()

    def finish_inputs(g):
        for d in range(1, NY):
            s2_copy(g, d).wait_recv()
        cross = s2[g] + s2r[g, 0] + s2r[g, 1] + s2r[g, 2]
        inv = inv_t[...]
        factor = cross * (inv * inv * inv) * (1.0 / FULL)
        for m in range(g * MG, (g + 1) * MG):
            for j in range(8):
                at = m * 8 + j
                fb[m, j * 8 : j * 8 + 8, :] = jnp.broadcast_to(factor[:, at : at + 1], (8, HEAD))
            rows = slice(m * ROWS, (m + 1) * ROWS)
            for k in range(HEADS):
                o = (sv[k, rows, :] - xp[k, rows, :] * fb[m]).astype(BF16)
                igv[m, :, k * HEAD : (k + 1) * HEAD] = dot(perm_back, o).astype(BF16)

    def gate_open():
        @pl.when(sec == 0)
        def _():
            pl.semaphore_signal(gate, inc=1, device_id=other_core, device_id_type=MESH)

    @pl.when(sec == 1)
    def _():
        for g in range(GROUPS):
            state_carry(g)
            q_carry(g)
            for k in range(HEADS):
                grad_head(k, g * MG, (g + 1) * MG)
            cross_sums(g)
        for k in range(HEADS):
            weight_head(k)

    @pl.when(sec == 0)
    def _():
        for g in range(GROUPS):
            q_carry(g)
        for k in range(HEADS):
            grad_head(k, 0, MICRO)
            weight_head(k)
        for g in range(GROUPS):
            cross_sums(g)

    @pl.when(sec == 1)
    def _():
        for g in range(GROUPS):
            finish_inputs(g)
            up_copy(g).start()

    own_head(1)
    gate_open()
    own_head(2)
    head0_z()
    own_head(3)

    vector_sums()

    @pl.when(sec == 0)
    def _():
        for g in range(GROUPS):
            finish_inputs(g)

    head0_x()

    for k in range(1, HEADS):
        for d in range(1, NZ):
            rz_copy(k, d).wait_recv()
        total = rs1[k, z_at].astype(F32)
        for d in range(1, NZ):
            total = total + rz[k, d - 1].astype(F32)
        wgo[x_at, z_at, k] = total.astype(BF16)
        if k > 1:
            for d in FAR_Z:
                az_copy(k - 2, d).start()

    @pl.when(sec == 1)
    def _():
        head0_spread()

    for d in range(1, NZ):
        vz_copy(d).wait_recv()
    v_sum = vzs[...]
    for d in range(1, NZ):
        v_sum = v_sum + vzr[d - 1]
    vxs[...] = v_sum
    for d in FAR_4:
        vx_copy(d).start()

    @pl.when(sec == 1)
    def _():
        pl.semaphore_wait(gate, 1)

    for p in range(2):
        spread(p, 0)

    @pl.when(sec == 0)
    def _():
        head0_spread()

    for near in ((1, 7), (2, 6), (3, 5)):
        for p in range(2):
            for d in near:
                spread(p, d)

    for p in range(2):
        spread(p, 4)

    for d in range(1, NX):
        vx_copy(d).wait_recv()
    v_sum = vxs[...]
    for d in range(1, NX):
        v_sum = v_sum + vxr[d - 1]
    vec_ref[...] = v_sum

    for d in range(1, NZ):
        bz0_copy(d, True).wait_recv()
    for p in range(2):
        for d in range(NZ):
            for e in range(1, NX):
                ax_copy(p, e, d, True).wait_recv()

    for c in s1_copies:
        c.wait_send()
    for g in range(GROUPS):
        for d in range(1, NZ):
            fz(g, d).wait_send()
            bz(g, d).wait_send()
        for d in range(1, NX):
            fx(g, d).wait_send()
            bx(g, d).wait_send()
        for d in range(1, NY):
            s2_copy(g, d).wait_send()

    @pl.when(sec == 1)
    def _():
        for g in range(GROUPS):
            up_copy(g).wait_send()

    for d in range(1, NZ):
        vz_copy(d).wait_send()
    for d in range(1, NX):
        vx_copy(d).wait_send()
    for d in range(1, NX):
        x0_copy(d).wait_send()
        bx0_copy(d).wait_send()
    for d in range(1, NZ):
        z0_copy(d).wait_send()
        bz0_copy(d).wait_send()
    for k in range(1, HEADS):
        for d in range(1, NX):
            rx_copy(k, d).wait_send()
        for d in range(1, NZ):
            rz_copy(k, d).wait_send()
    for p in range(2):
        for d in range(1, NZ):
            az_copy(p, d).wait_send()
        for d in range(NZ):
            for e in range(1, NX):
                ax_copy(p, e, d).wait_send()


def hand_out(ig_ref, w_ref, v_ref, ig_out, rate_out, input_out, v_out, staged, v_staged, sem):
    scale = 1.0 / math.sqrt(MICRO * ROWS * NX * NZ)
    copies = [pltpu.make_async_copy(ig_ref, ig_out.at[0], sem.at[0])]
    copies[0].start()
    v_staged[...] = v_ref[...] * scale
    copies.append(pltpu.make_async_copy(v_staged, v_out, sem.at[1]))
    copies[1].start()
    for k in range(HEADS):
        for c in range(NX):
            for z in range(NZ):
                top = c * ROWS + (z // 2) * 16
                staged[z % 2, k, top : top + 16, :] = w_ref[c, z, k].astype(F32) * scale
        for half, out in enumerate((rate_out, input_out)):
            copies.append(pltpu.make_async_copy(staged.at[half, k], out.at[0, k], sem.at[2 + 2 * k + half]))
            copies[-1].start()
    for c in copies:
        c.wait()


def on_device(*arguments):
    tokens = MICRO * ROWS
    wide = pltpu.VMEM((HEADS, tokens, HEAD), F32)
    seg = pltpu.VMEM((HEADS, MICRO * 8, HEAD), F32)
    dma = pltpu.SemaphoreType.DMA

    def tiles(*lead, dtype=F32):
        return pltpu.VMEM((*lead, 8, 128), dtype)

    row = pltpu.VMEM((1, WIDTH), F32)
    scratch = [
        row, row, row, row, pltpu.SMEM((MICRO, 3), jnp.int32),
        pltpu.VMEM((MICRO, ROWS, WIDTH), BF16),
        pltpu.VMEM((MICRO, ROWS, WIDTH), BF16),
        pltpu.VMEM((HEADS, HEAD, HEAD), BF16),
        pltpu.VMEM((HEADS, HEAD, HEAD), BF16),
        wide,
        pltpu.VMEM((HEADS, tokens, HEAD), BF16),
        wide, wide, wide, wide, wide, wide,
        wide, wide, wide,
        pltpu.VMEM((HEADS, tokens, 2 * HEAD), BF16),
        pltpu.VMEM((MICRO, ROWS, HEAD), F32),
        pltpu.VMEM((MICRO, ROWS, HEAD), F32),
        tiles(),
        pltpu.VMEM((MICRO, ROWS, HEAD), F32),
        seg, seg, seg, seg, seg,
        tiles(MICRO, 2), tiles(MICRO), tiles(NZ - 1, MICRO),
        tiles(MICRO, 2, dtype=BF16), tiles(NZ - 1, MICRO, 2, dtype=BF16),
        tiles(MICRO, 2, dtype=BF16), tiles(NX - 1, MICRO, 2, dtype=BF16),
        tiles(MICRO, dtype=BF16), tiles(NZ - 1, MICRO, dtype=BF16),
        tiles(MICRO, dtype=BF16), tiles(NX - 1, MICRO, dtype=BF16),
        tiles(MICRO), tiles(MICRO), tiles(MICRO, 2), tiles(MICRO),
        tiles(), tiles(NY - 1),
        pltpu.VMEM((MICRO, ROWS, 128), F32),
        tiles(GROUPS), tiles(GROUPS, NY - 1),
        pltpu.VMEM((3, HEADS, 8, HEAD), F32),
        tiles(3), tiles(NZ - 1, 3), tiles(3), tiles(NX - 1, 3),
        pltpu.VMEM((HEADS, HEAD, tokens), BF16),
        pltpu.VMEM((HEADS, NX, NZ, 16, HEAD), BF16),
        pltpu.VMEM((HEADS, NX - 1, NZ, 16, HEAD), BF16),
        pltpu.VMEM((HEADS, NZ, 16, HEAD), BF16),
        pltpu.VMEM((HEADS, NZ - 1, 16, HEAD), BF16),
        pltpu.VMEM((NZ - 1, NX, 16, HEAD), BF16),
        pltpu.VMEM((NX, 16, HEAD), BF16),
        pltpu.VMEM((NX - 1, 16, HEAD), BF16),
        dma((9,)),
    ]
    scratch += [dma((NY - 1,))] * 2 + [dma((GROUPS, NY - 1))] * 2
    scratch += ([dma((GROUPS, NZ - 1))] * 2 + [dma((GROUPS, NX - 1))] * 2) * 2
    scratch += [dma((GROUPS,))] * 2
    scratch += [dma((NZ - 1,))] * 2 + [dma((NX - 1,))] * 2
    scratch += [dma((HEADS, NX - 1))] * 2 + [dma((HEADS, NZ - 1))] * 2 + [dma((2, NZ - 1))] * 2
    scratch += [dma((2, NX - 1, NZ))] * 2 + [pltpu.SemaphoreType.REGULAR]
    scratch += [dma((NZ - 1,))] * 2 + [dma((NX - 1,))] * 4 + [dma((NZ - 1,))] * 2

    hbm = pl.BlockSpec(memory_space=pltpu.HBM)
    vmem = pl.BlockSpec(memory_space=pltpu.VMEM)
    input_grads, weight_sums, vector_sums = pl.pallas_call(
        body,
        out_shape=(
            jax.ShapeDtypeStruct((MICRO, ROWS, WIDTH), BF16),
            jax.ShapeDtypeStruct((NX, NZ, HEADS, 16, HEAD), BF16),
            jax.ShapeDtypeStruct((3, 8, 128), F32),
        ),
        in_specs=[hbm] * 9,
        out_specs=(vmem, vmem, vmem),
        scratch_shapes=scratch,
        compiler_params=pltpu.CompilerParams(
            collective_id=0, has_side_effects=True, vmem_limit_bytes=48 << 20
        ),
        name="rglru_backward",
    )(*(pltpu.with_memory_space_constraint(v, pltpu.HBM) for v in arguments))
    square = jax.ShapeDtypeStruct((1, HEADS, HEAD, HEAD), F32)
    input_grads, rate_grad, input_grad, vector_grads = pl.pallas_call(
        hand_out,
        out_shape=(
            jax.ShapeDtypeStruct((1, MICRO, ROWS, WIDTH), BF16), square, square,
            jax.ShapeDtypeStruct((3, 8, 128), F32),
        ),
        in_specs=[vmem] * 3,
        out_specs=(hbm, hbm, hbm, hbm),
        scratch_shapes=[
            pltpu.VMEM((2, HEADS, HEAD, HEAD), F32), pltpu.VMEM((3, 8, 128), F32), dma((2 + 2 * HEADS,)),
        ],
        compiler_params=pltpu.CompilerParams(vmem_limit_bytes=8 << 20),
        name="hand_out",
    )(input_grads, weight_sums, vector_sums)
    return (input_grads, rate_grad, input_grad, vector_grads.reshape(1, 3, WIDTH))


def solution(mesh):
    in_specs = (
        P("section", None, "seq", "chan"),
        P(None, "seq", "chan"),
        P("section", "chan", None, None),
        P("section", "chan", None, None),
        P("section", "chan"),
        P("section", "chan"),
        P("section", "chan"),
        P("section", "chan"),
        P(),
    )
    out_specs = (
        P("section", None, "seq", "chan"),
        P("section", "chan", None, None),
        P("section", "chan", None, None),
        P("section", None, "chan"),
    )
    return jax.shard_map(
        on_device, mesh=mesh, in_specs=in_specs, out_specs=out_specs, check_vma=False
    )
```

```python
import math

import jax
import jax.numpy as jnp
from jax import lax
from jax.experimental import pallas as pl
from jax.experimental.pallas import tpu as pltpu
from jax.sharding import PartitionSpec as P

F32 = jnp.float32
BF16 = jnp.bfloat16
NX, NZ, NY = 4, 8, 4
MICRO, ROWS, WIDTH = 4, 64, 1024
HEADS, HEAD = 4, 256
FULL = WIDTH * NY
GROUPS = 2
MG = MICRO // GROUPS
GR = MG * ROWS
MESH = pl.DeviceIdType.MESH
FAR_Z = (4, 3, 5, 2, 6, 1, 7)
FAR_4 = (2, 1, 3)


def dot(a, b):
    return jnp.dot(a, b, preferred_element_type=F32)


def dot_t(a, b):
    return lax.dot_general(a, b, (((1,), (1,)), ((), ())), preferred_element_type=F32)


def sublane(shape):
    return lax.broadcasted_iota(jnp.int32, shape, 0)


def lane(shape):
    return lax.broadcasted_iota(jnp.int32, shape, 1)


def log1p_of(v):
    series = v * (1.0 - v * (0.5 - v * (1.0 / 3.0 - v * (0.25 - v * 0.2))))
    return jnp.where(v < 0.03125, series, jnp.log(1.0 + v))


def log_of(a):
    return jnp.log(jnp.maximum(a, 1e-37))


def decay_of(tile):
    wide = tile.astype(F32)
    return jnp.where(wide < -80.0, 0.0, jnp.exp(wide))


def body(
    x_hbm, up_hbm, rw_hbm, iw_hbm, rb_hbm, ib_hbm, dp_hbm, gain_hbm, starts_hbm,
    igv, wgo, vec_ref,
    rb_ref, ib_ref, dp_ref, gain_ref, starts_ref,
    xv, upv, rwv, iwv, xp, nd, dec, drv, mi, rr, kk, cc, upp, sv, dg, gb, keep, invb, inv_t, fb,
    ea, eh, eba, ebq, pa_s, fzt, bzt, za, fzs, fzr, fxs, fxr, bzs, bzr, bxs, bxr, stin, qin, zpre, zsuf,
    s1, s1r, ca, s2, s2r, vacc, vzs, vzr, vxs, vxr,
    ndt, wgb, rx, rs1, rz, z0, t0, x0,
    loc_sem, s1_ss, s1_rs, s2_ss, s2_rs, fz_ss, fz_rs, fx_ss, fx_rs, bz_ss, bz_rs, bx_ss, bx_rs,
    up_ss, up_rs, vz_ss, vz_rs, vx_ss, vx_rs, rx_ss, rx_rs, rz_ss, rz_rs, az_ss, az_rs, ax_ss, ax_rs, gate,
    z0_ss, z0_rs, x0_ss, x0_rs, bx0_ss, bx0_rs, bz0_ss, bz0_rs,
):
    sec = lax.axis_index("section")
    seq = lax.axis_index("seq")
    chan = lax.axis_index("chan")
    x_at = seq // NZ
    z_at = seq % NZ

    def z_peer(d):
        return {"seq": x_at * NZ + (z_at + d) % NZ}

    def x_peer(d):
        return {"seq": ((x_at + d) % NX) * NZ + z_at}

    def y_peer(d):
        return {"chan": (chan + d) % NY}

    other_core = {"section": 1 - sec}

    def remote(src, dst, ss, rs, to):
        return pltpu.make_async_remote_copy(
            src_ref=src, dst_ref=dst, send_sem=ss, recv_sem=rs, device_id=to, device_id_type=MESH
        )

    loads = [
        pltpu.make_async_copy(x_hbm.at[0], xv, loc_sem.at[0]),
        pltpu.make_async_copy(starts_hbm, starts_ref, loc_sem.at[4]),
    ]
    w_loads = [
        pltpu.make_async_copy(gain_hbm, gain_ref, loc_sem.at[5]),
        pltpu.make_async_copy(dp_hbm, dp_ref, loc_sem.at[6]),
        pltpu.make_async_copy(rb_hbm, rb_ref, loc_sem.at[7]),
        pltpu.make_async_copy(ib_hbm, ib_ref, loc_sem.at[8]),
        pltpu.make_async_copy(rw_hbm.at[0], rwv, loc_sem.at[1]),
        pltpu.make_async_copy(iw_hbm.at[0], iwv, loc_sem.at[2]),
    ]
    up_load = pltpu.make_async_copy(up_hbm, upv, loc_sem.at[3])
    for c in loads + w_loads:
        c.start()

    @pl.when(sec == 1)
    def _():
        up_load.start()

    barrier = pltpu.get_barrier_semaphore()
    peers = [z_peer(d) for d in range(1, NZ)] + [x_peer(d) for d in range(1, NX)]
    peers += [y_peer(d) for d in range(1, NY)] + [other_core]
    for to in peers:
        pl.semaphore_signal(barrier, inc=1, device_id=to, device_id_type=MESH)

    r_i = sublane((ROWS, ROWS))
    t_i = lane((ROWS, ROWS))
    perm = jnp.where(t_i == (r_i % 8) * 8 + r_i // 8, 1.0, 0.0).astype(BF16)
    perm_back = jnp.where(r_i == (t_i % 8) * 8 + t_i // 8, 1.0, 0.0).astype(BF16)

    vacc[...] = jnp.zeros_like(vacc)
    ca[...] = jnp.zeros_like(ca)


    for c in loads:
        c.wait()
    lane_t = lane((8, 128))
    tile = jnp.zeros((8, 128), F32)
    for m in range(MICRO):
        x_m = dot(perm, xv[m])
        acc = jnp.zeros((ROWS, 128), F32)
        for k in range(HEADS):
            x_k = x_m[:, k * HEAD : (k + 1) * HEAD]
            xp[k, m * ROWS : (m + 1) * ROWS, :] = x_k
            sq = x_k * x_k
            acc = acc + (sq[:, :128] + sq[:, 128:])
        for j in range(8):
            col = jnp.sum(acc[j * 8 : j * 8 + 8], axis=1, keepdims=True)
            tile = jnp.where(lane_t == m * 8 + j, col, tile)
    s1[...] = tile
    pl.semaphore_wait(barrier, len(peers))
    s1_copies = [
        remote(s1, s1r.at[d - 1], s1_ss.at[d - 1], s1_rs.at[d - 1], y_peer(d)) for d in range(1, NY)
    ]
    for c in s1_copies:
        c.start()
    r_w = sublane((ROWS, HEAD))
    position = seq * ROWS + (r_w % 8) * 8 + r_w // 8
    for m in range(MICRO):
        reset = position == 0
        for d in range(3):
            reset = jnp.logical_or(reset, position == starts_ref[m, d])
        keep[m] = jnp.where(reset, 0.0, 1.0)
    for c in w_loads:
        c.wait()
    for c in s1_copies:
        c.wait_recv()
    inv_tile = lax.rsqrt((s1[...] + s1r[0] + s1r[1] + s1r[2]) / FULL + 1e-06)
    inv_t[...] = inv_tile
    for m in range(MICRO):
        for j in range(8):
            at = m * 8 + j
            invb[m, j * 8 : j * 8 + 8, :] = jnp.broadcast_to(inv_tile[:, at : at + 1], (8, HEAD))

    sub = sublane((8, HEAD))

    def scan_up(a, h):
        for sh in (1, 2, 4):
            ok = sub >= sh
            h = h + a * jnp.where(ok, pltpu.roll(h, sh, 0), 0.0)
            a = a * jnp.where(ok, pltpu.roll(a, sh, 0), 1.0)
        return a, h

    def scan_down(a, h):
        for sh in (1, 2, 4):
            ok = sub < 8 - sh
            h = h + a * jnp.where(ok, pltpu.roll(h, 8 - sh, 0), 0.0)
            a = a * jnp.where(ok, pltpu.roll(a, 8 - sh, 0), 1.0)
        return a, h

    def to_tile(ref, index, k, row):
        for half in range(2):
            ref[(*index, pl.ds(k * 2 + half, 1), slice(None))] = row[:, half * 128 : half * 128 + 128]

    def from_tile(ref, index, k):
        return jnp.concatenate(
            [ref[(*index, pl.ds(k * 2 + half, 1), slice(None))] for half in range(2)], axis=1
        )

    def head_lanes(k):
        return pl.ds(pl.multiple_of(k * HEAD, HEAD), HEAD)

    def forward_head(g, k):
        gain = gain_ref[:, head_lanes(k)]
        rb = rb_ref[:, head_lanes(k)]
        ib = ib_ref[:, head_lanes(k)]
        v = dp_ref[:, head_lanes(k)]
        rate = -8.0 * (jnp.maximum(-v, 0.0) + log1p_of(jnp.exp(-jnp.abs(v))))
        for m in range(g * MG, (g + 1) * MG):
            rows = slice(m * ROWS, (m + 1) * ROWS)
            nd[k, rows, :] = (xp[k, rows, :] * invb[m] * gain).astype(BF16)
        grow = slice(g * GR, (g + 1) * GR)
        n_g = nd[k, grow, :]
        pre_r = dot(n_g, rwv[k])
        pre_i = dot(n_g, iwv[k])
        for m in range(g * MG, (g + 1) * MG):
            rows = slice(m * ROWS, (m + 1) * ROWS)
            own = slice((m - g * MG) * ROWS, (m - g * MG + 1) * ROWS)
            rg = 0.5 * jnp.tanh(0.5 * (pre_r[own] + rb)) + 0.5
            ig = 0.5 * jnp.tanh(0.5 * (pre_i[own] + ib)) + 0.5
            nw = n_g[own].astype(F32)
            kept = keep[m]
            ld = rate * rg
            e = jnp.exp(ld)
            gap = e * e
            em = jnp.tanh(-ld) * (1.0 + gap)
            em = jnp.maximum(em, 1e-06)
            rs = lax.rsqrt(em)
            mult = jnp.where(kept > 0.5, em * rs, 1.0)
            a = e * kept
            mig = mult * ig
            b = mig * nw
            dec[k, rows, :] = a
            drv[k, rows, :] = b
            mi[k, rows, :] = mig
            rr[k, rows, :] = kept * (ig * nw * gap * rs)
            kk[k, rows, :] = ld * (1.0 - rg)
            cc[k, rows, :] = b * (1.0 - ig)
            pa = a[:8]
            h = b[:8]
            for j in range(1, 8):
                a_j = a[j * 8 : j * 8 + 8]
                h = a_j * h + b[j * 8 : j * 8 + 8]
                pa = pa * a_j
            seg = slice(m * 8, m * 8 + 8)
            pa_s[k, seg, :] = pa
            a_in, h_in = scan_up(pa, h)
            ea[k, seg, :] = jnp.where(sub >= 1, pltpu.roll(a_in, 1, 0), 1.0)
            eh[k, seg, :] = jnp.where(sub >= 1, pltpu.roll(h_in, 1, 0), 0.0)
            to_tile(fzt, (m, 0), k, a_in[7:8])
            to_tile(fzt, (m, 1), k, h_in[7:8])

    def group(g):
        return pl.ds(g * MG, MG)

    def fz(g, d):
        return remote(
            fzs.at[group(g)], fzr.at[d - 1, group(g)], fz_ss.at[g, d - 1], fz_rs.at[g, d - 1], z_peer(d)
        )

    def fx(g, d):
        return remote(
            fxs.at[group(g)], fxr.at[d - 1, group(g)], fx_ss.at[g, d - 1], fx_rs.at[g, d - 1], x_peer(d)
        )

    def bz(g, d):
        return remote(
            bzs.at[group(g)], bzr.at[d - 1, group(g)], bz_ss.at[g, d - 1], bz_rs.at[g, d - 1], z_peer(d)
        )

    def bx(g, d):
        return remote(
            bxs.at[group(g)], bxr.at[d - 1, group(g)], bx_ss.at[g, d - 1], bx_rs.at[g, d - 1], x_peer(d)
        )

    def up_copy(m):
        return remote(igv.at[m], upv.at[m], up_ss.at[m], up_rs.at[m], other_core)

    def back_local(g, arriving):
        for m in range(g * MG, (g + 1) * MG):
            if arriving:
                up_copy(m).wait_recv()
            u_m = dot(perm, upv[m])
            for k in range(HEADS):
                upp[k, m * ROWS : (m + 1) * ROWS, :] = u_m[:, k * HEAD : (k + 1) * HEAD]
            for k in range(HEADS):
                q = jnp.zeros((8, HEAD), F32)
                for j in range(7, -1, -1):
                    at = slice(m * ROWS + j * 8, m * ROWS + j * 8 + 8)
                    q = dec[k, at, :] * (upp[k, at, :] + q)
                seg = slice(m * 8, m * 8 + 8)
                a_in, q_in = scan_down(pa_s[k, seg, :], q)
                eba[k, seg, :] = jnp.where(sub < 7, pltpu.roll(a_in, 7, 0), 1.0)
                ebq[k, seg, :] = jnp.where(sub < 7, pltpu.roll(q_in, 7, 0), 0.0)
                to_tile(bzt, (m,), k, q_in[0:1])
        for m in range(g * MG, (g + 1) * MG):
            bzs[m] = bzt[m].astype(BF16)
        for d in FAR_Z:
            bz(g, d).start()

    @pl.when(sec == 1)
    def _():
        up_load.wait()

    for g in range(GROUPS):
        for k in range(HEADS):
            forward_head(g, k)
        for m in range(g * MG, (g + 1) * MG):
            fzs[m, 0] = log_of(fzt[m, 0]).astype(BF16)
            fzs[m, 1] = fzt[m, 1].astype(BF16)
        for d in FAR_Z:
            fz(g, d).start()

        @pl.when(sec == 1)
        def _(g=g):
            back_local(g, False)

    def turn_k(k, carry):
        ndt[k] = nd[k].T
        return carry

    lax.fori_loop(0, HEADS, turn_k, 0)

    def forward_totals(g):
        for d in range(1, NZ):
            fz(g, d).wait_recv()
        for m in range(g * MG, (g + 1) * MG):
            a_own, h_own = fzt[m, 0], fzt[m, 1]
            a_pre, h_pre = jnp.ones((8, 128), F32), jnp.zeros((8, 128), F32)
            a_suf, h_suf = a_pre, h_pre
            for d in range(1, NZ):
                ok = z_at >= d
                h_pre = h_pre + a_pre * jnp.where(ok, fzr[d - 1, m, 1].astype(F32), 0.0)
                a_d = decay_of(fzr[d - 1, m, 0])
                za[d - 1, m] = a_d
                a_pre = a_pre * jnp.where(ok, a_d, 1.0)
            for d in range(1, NZ):
                ok = z_at + d < NZ
                a_d = jnp.where(ok, za[NZ - d - 1, m], 1.0)
                h_suf = jnp.where(ok, fzr[NZ - d - 1, m, 1].astype(F32), 0.0) + a_d * h_suf
                a_suf = a_suf * a_d
            zpre[m, 0] = a_pre
            zpre[m, 1] = h_pre
            zsuf[m] = a_suf
            fxs[m, 0] = log_of(a_pre * a_own * a_suf).astype(BF16)
            fxs[m, 1] = (h_suf + a_suf * (h_own + a_own * h_pre)).astype(BF16)
        for d in FAR_4:
            fx(g, d).start()

    def backward_totals(g):
        for d in range(1, NZ):
            bz(g, d).wait_recv()
        for m in range(g * MG, (g + 1) * MG):
            a_run, q_run = jnp.ones((8, 128), F32), jnp.zeros((8, 128), F32)
            for d in range(1, NZ):
                ok = z_at + d < NZ
                q_run = q_run + a_run * jnp.where(ok, bzr[NZ - d - 1, m].astype(F32), 0.0)
                a_run = a_run * jnp.where(ok, za[NZ - d - 1, m], 1.0)
            qin[m] = q_run
            total = bzt[m] + fzt[m, 0] * q_run
            for d in range(1, NZ):
                ok = z_at >= d
                total = jnp.where(ok, bzr[d - 1, m].astype(F32) + za[d - 1, m] * total, total)
            bxs[m] = total.astype(BF16)
        for d in FAR_4:
            bx(g, d).start()

    def state_carry(g):
        for d in range(1, NX):
            fx(g, d).wait_recv()
        for m in range(g * MG, (g + 1) * MG):
            a_run, h_run = jnp.ones((8, 128), F32), jnp.zeros((8, 128), F32)
            for d in range(1, NX):
                ok = x_at >= d
                h_run = h_run + a_run * jnp.where(ok, fxr[d - 1, m, 1].astype(F32), 0.0)
                a_run = a_run * jnp.where(ok, decay_of(fxr[d - 1, m, 0]), 1.0)
            stin[m] = zpre[m, 1] + zpre[m, 0] * h_run

    for g in range(GROUPS):
        forward_totals(g)

        @pl.when(sec == 1)
        def _(g=g):
            backward_totals(g)

    @pl.when(sec == 0)
    def _():
        for g in range(GROUPS):
            state_carry(g)
        for g in range(GROUPS):
            back_local(g, True)

    @pl.when(sec == 0)
    def _():
        for g in range(GROUPS):
            backward_totals(g)

    def s2_copy(g, d):
        return remote(s2.at[g], s2r.at[g, d - 1], s2_ss.at[g, d - 1], s2_rs.at[g, d - 1], y_peer(d))

    def q_carry(g):
        for d in range(1, NX):
            bx(g, d).wait_recv()
        for m in range(g * MG, (g + 1) * MG):
            a_run, q_run = jnp.ones((8, 128), F32), jnp.zeros((8, 128), F32)
            for d in range(1, NX):
                ok = x_at + d < NX
                q_run = q_run + a_run * jnp.where(ok, bxr[NX - d - 1, m].astype(F32), 0.0)
                a_run = a_run * jnp.where(ok, decay_of(fxr[NX - d - 1, m, 0]), 1.0)
            qin[m] = qin[m] + zsuf[m] * q_run

    def grad_head(k, low, high):
        gain = gain_ref[:, head_lanes(k)]
        v0 = vacc[0, k]
        v1 = vacc[1, k]
        v2 = vacc[2, k]
        for m in range(low, high):
            seg = slice(m * 8, m * 8 + 8)
            prev = eh[k, seg, :] + ea[k, seg, :] * from_tile(stin, (m,), k)
            q = ebq[k, seg, :] + eba[k, seg, :] * from_tile(qin, (m,), k)
            terms = []
            for j in range(8):
                at = slice(m * ROWS + j * 8, m * ROWS + j * 8 + 8)
                t = dec[k, at, :] * prev
                terms.append((t - rr[k, at, :]) * kk[k, at, :])
                prev = t + drv[k, at, :]
            rate_rows, input_rows = [None] * 8, [None] * 8
            for j in range(7, -1, -1):
                at = slice(m * ROWS + j * 8, m * ROWS + j * 8 + 8)
                sg = upp[k, at, :] + q
                q = dec[k, at, :] * sg
                rate_rows[j] = sg * terms[j]
                input_rows[j] = sg * cc[k, at, :]
                dg[k, at, :] = sg * mi[k, at, :]
            gr = jnp.concatenate(rate_rows, axis=0).astype(BF16)
            gi = jnp.concatenate(input_rows, axis=0).astype(BF16)
            rows = slice(m * ROWS, (m + 1) * ROWS)
            gb[k, rows, :HEAD] = gr
            gb[k, rows, HEAD:] = gi
            v0 = v0 + jnp.sum(gr.astype(F32).reshape(8, 8, HEAD), axis=0)
            v1 = v1 + jnp.sum(gi.astype(F32).reshape(8, 8, HEAD), axis=0)
        grow = slice(low * ROWS, high * ROWS)
        bp = dot_t(gb[k, grow, :HEAD], rwv[k]) + dot_t(gb[k, grow, HEAD:], iwv[k])
        for m in range(low, high):
            rows = slice(m * ROWS, (m + 1) * ROWS)
            own = slice((m - low) * ROWS, (m - low + 1) * ROWS)
            gn = dg[k, rows, :] + bp[own]
            w = gn * xp[k, rows, :]
            v2 = v2 + jnp.sum((w * invb[m]).reshape(8, 8, HEAD), axis=0)
            wg = w * gain
            ca[m] += wg[:, :128] + wg[:, 128:]
            sv[k, rows, :] = upp[k, rows, :] + gn * gain * invb[m]
        vacc[0, k] = v0
        vacc[1, k] = v1
        vacc[2, k] = v2

    def cross_sums(g):
        tile = jnp.zeros((8, 128), F32)
        for m in range(g * MG, (g + 1) * MG):
            for j in range(8):
                col = jnp.sum(ca[m, j * 8 : j * 8 + 8, :], axis=1, keepdims=True)
                tile = jnp.where(lane_t == m * 8 + j, col, tile)
        s2[g] = tile
        for d in FAR_4:
            s2_copy(g, d).start()

    def rx_copy(k, d):
        return remote(
            wgb.at[k, (x_at + d) % NX], rx.at[k, d - 1], rx_ss.at[k, d - 1], rx_rs.at[k, d - 1], x_peer(d)
        )

    def z0_copy(d):
        return remote(
            wgb.at[0, :, (z_at + d) % NZ], z0.at[d - 1], z0_ss.at[d - 1], z0_rs.at[d - 1], z_peer(d)
        )

    def x0_copy(d):
        return remote(t0.at[(x_at + d) % NX], x0.at[d - 1], x0_ss.at[d - 1], x0_rs.at[d - 1], x_peer(d))

    def bx0_copy(d, arrival=False):
        ref = wgo.at[(x_at + NX - d) % NX if arrival else x_at, z_at, 0]
        return remote(ref, ref, bx0_ss.at[d - 1], bx0_rs.at[d - 1], x_peer(d))

    def bz0_copy(d, arrival=False):
        ref = wgo.at[:, (z_at + NZ - d) % NZ if arrival else z_at, 0]
        return remote(ref, ref, bz0_ss.at[d - 1], bz0_rs.at[d - 1], z_peer(d))

    def head0_z():
        for d in range(1, NZ):
            z0_copy(d).wait_recv()
        total = wgb[0, :, z_at].astype(F32)
        for d in range(1, NZ):
            total = total + z0[d - 1].astype(F32)
        t0[...] = total.astype(BF16)
        for d in FAR_4:
            x0_copy(d).start()

    def head0_x():
        for d in range(1, NX):
            x0_copy(d).wait_recv()
        total = t0[x_at].astype(F32)
        for d in range(1, NX):
            total = total + x0[d - 1].astype(F32)
        wgo[x_at, z_at, 0] = total.astype(BF16)
        for d in FAR_4:
            bx0_copy(d).start()

    def head0_spread():
        for d in range(1, NX):
            bx0_copy(d, True).wait_recv()
        for d in FAR_Z:
            bz0_copy(d).start()

    def weight_head(k):
        w_k = dot(ndt[k], gb[k]).astype(BF16)
        for c in range(NX):
            for z in range(NZ):
                top = c * ROWS + (z // 2) * 16
                wgb[k, c, z] = w_k[top : top + 16, (z % 2) * HEAD : (z % 2) * HEAD + HEAD]
        if k == 0:
            for d in FAR_Z:
                z0_copy(d).start()
        else:
            for d in FAR_4:
                rx_copy(k, d).start()

    def rz_copy(k, d):
        return remote(
            rs1.at[k, (z_at + d) % NZ], rz.at[k, d - 1], rz_ss.at[k, d - 1], rz_rs.at[k, d - 1], z_peer(d)
        )

    def piece(x, z, p):
        return wgo.at[x, z, pl.ds(1, 2) if p == 0 else pl.ds(3, 1)]

    def from_z(d):
        return (z_at + NZ - d) % NZ

    def az_copy(p, d, arrival=False):
        ref = piece(x_at, from_z(d) if arrival else z_at, p)
        return remote(ref, ref, az_ss.at[p, d - 1], az_rs.at[p, d - 1], z_peer(d))

    def ax_copy(p, e, d, arrival=False):
        ref = piece((x_at + NX - e) % NX if arrival else x_at, from_z(d), p)
        return remote(ref, ref, ax_ss.at[p, e - 1, d], ax_rs.at[p, e - 1, d], x_peer(e))

    def spread(p, d):
        if d:
            az_copy(p, d, True).wait_recv()
        for e in FAR_4:
            ax_copy(p, e, d).start()

    def own_head(k):
        for d in range(1, NX):
            rx_copy(k, d).wait_recv()
        total = wgb[k, x_at].astype(F32)
        for d in range(1, NX):
            total = total + rx[k, d - 1].astype(F32)
        rs1[k] = total.astype(BF16)
        for d in FAR_Z:
            rz_copy(k, d).start()

    def vz_copy(d):
        return remote(vzs, vzr.at[d - 1], vz_ss.at[d - 1], vz_rs.at[d - 1], z_peer(d))

    def vx_copy(d):
        return remote(vxs, vxr.at[d - 1], vx_ss.at[d - 1], vx_rs.at[d - 1], x_peer(d))

    def vector_sums():
        for i in range(3):
            for k in range(HEADS):
                to_tile(vzs, (i,), k, jnp.sum(vacc[i, k], axis=0, keepdims=True))
        for d in FAR_Z:
            vz_copy(d).start()

    def finish_inputs(g, send):
        for d in range(1, NY):
            s2_copy(g, d).wait_recv()
        cross = s2[g] + s2r[g, 0] + s2r[g, 1] + s2r[g, 2]
        inv = inv_t[...]
        factor = cross * (inv * inv * inv) * (1.0 / FULL)
        for m in range(g * MG, (g + 1) * MG):
            for j in range(8):
                at = m * 8 + j
                fb[m, j * 8 : j * 8 + 8, :] = jnp.broadcast_to(factor[:, at : at + 1], (8, HEAD))
            rows = slice(m * ROWS, (m + 1) * ROWS)
            for k in range(HEADS):
                o = (sv[k, rows, :] - xp[k, rows, :] * fb[m]).astype(BF16)
                igv[m, :, k * HEAD : (k + 1) * HEAD] = dot(perm_back, o).astype(BF16)
            if send:
                up_copy(m).start()

    def gate_open():
        @pl.when(sec == 0)
        def _():
            pl.semaphore_signal(gate, inc=1, device_id=other_core, device_id_type=MESH)

    @pl.when(sec == 1)
    def _():
        for g in range(GROUPS):
            state_carry(g)
            q_carry(g)
            for k in range(HEADS):
                grad_head(k, g * MG, (g + 1) * MG)
            cross_sums(g)
        for k in range(HEADS):
            weight_head(k)

    @pl.when(sec == 0)
    def _():
        for g in range(GROUPS):
            q_carry(g)
        for k in range(HEADS):
            grad_head(k, 0, MICRO)
            weight_head(k)
        for g in range(GROUPS):
            cross_sums(g)

    @pl.when(sec == 1)
    def _():
        for g in range(GROUPS):
            finish_inputs(g, True)

    own_head(1)
    gate_open()
    own_head(2)
    head0_z()
    own_head(3)

    vector_sums()

    @pl.when(sec == 0)
    def _():
        for g in range(GROUPS):
            finish_inputs(g, False)

    head0_x()

    for k in range(1, HEADS):
        for d in range(1, NZ):
            rz_copy(k, d).wait_recv()
        total = rs1[k, z_at].astype(F32)
        for d in range(1, NZ):
            total = total + rz[k, d - 1].astype(F32)
        wgo[x_at, z_at, k] = total.astype(BF16)
        if k > 1:
            for d in FAR_Z:
                az_copy(k - 2, d).start()

    @pl.when(sec == 1)
    def _():
        head0_spread()

    for d in range(1, NZ):
        vz_copy(d).wait_recv()
    v_sum = vzs[...]
    for d in range(1, NZ):
        v_sum = v_sum + vzr[d - 1]
    vxs[...] = v_sum
    for d in FAR_4:
        vx_copy(d).start()

    @pl.when(sec == 1)
    def _():
        pl.semaphore_wait(gate, 1)

    for p in range(2):
        spread(p, 0)

    @pl.when(sec == 0)
    def _():
        head0_spread()

    for near in ((1, 7), (2, 6), (3, 5)):
        for p in range(2):
            for d in near:
                spread(p, d)

    for p in range(2):
        spread(p, 4)

    for d in range(1, NX):
        vx_copy(d).wait_recv()
    v_sum = vxs[...]
    for d in range(1, NX):
        v_sum = v_sum + vxr[d - 1]
    vec_ref[...] = v_sum

    for d in range(1, NZ):
        bz0_copy(d, True).wait_recv()
    for p in range(2):
        for d in range(NZ):
            for e in range(1, NX):
                ax_copy(p, e, d, True).wait_recv()

    for c in s1_copies:
        c.wait_send()
    for g in range(GROUPS):
        for d in range(1, NZ):
            fz(g, d).wait_send()
            bz(g, d).wait_send()
        for d in range(1, NX):
            fx(g, d).wait_send()
            bx(g, d).wait_send()
        for d in range(1, NY):
            s2_copy(g, d).wait_send()

    @pl.when(sec == 1)
    def _():
        for m in range(MICRO):
            up_copy(m).wait_send()

    for d in range(1, NZ):
        vz_copy(d).wait_send()
    for d in range(1, NX):
        vx_copy(d).wait_send()
    for d in range(1, NX):
        x0_copy(d).wait_send()
        bx0_copy(d).wait_send()
    for d in range(1, NZ):
        z0_copy(d).wait_send()
        bz0_copy(d).wait_send()
    for k in range(1, HEADS):
        for d in range(1, NX):
            rx_copy(k, d).wait_send()
        for d in range(1, NZ):
            rz_copy(k, d).wait_send()
    for p in range(2):
        for d in range(1, NZ):
            az_copy(p, d).wait_send()
        for d in range(NZ):
            for e in range(1, NX):
                ax_copy(p, e, d).wait_send()


def hand_out(ig_ref, w_ref, v_ref, ig_out, rate_out, input_out, v_out, staged, v_staged, sem):
    scale = 1.0 / math.sqrt(MICRO * ROWS * NX * NZ)
    copies = [pltpu.make_async_copy(ig_ref, ig_out.at[0], sem.at[0])]
    copies[0].start()
    v_staged[...] = v_ref[...] * scale
    copies.append(pltpu.make_async_copy(v_staged, v_out, sem.at[1]))
    copies[1].start()
    for k in range(HEADS):
        for c in range(NX):
            for z in range(NZ):
                top = c * ROWS + (z // 2) * 16
                staged[z % 2, k, top : top + 16, :] = w_ref[c, z, k].astype(F32) * scale
        for half, out in enumerate((rate_out, input_out)):
            copies.append(pltpu.make_async_copy(staged.at[half, k], out.at[0, k], sem.at[2 + 2 * k + half]))
            copies[-1].start()
    for c in copies:
        c.wait()


def on_device(*arguments):
    tokens = MICRO * ROWS
    wide = pltpu.VMEM((HEADS, tokens, HEAD), F32)
    seg = pltpu.VMEM((HEADS, MICRO * 8, HEAD), F32)
    dma = pltpu.SemaphoreType.DMA

    def tiles(*lead, dtype=F32):
        return pltpu.VMEM((*lead, 8, 128), dtype)

    row = pltpu.VMEM((1, WIDTH), F32)
    scratch = [
        row, row, row, row, pltpu.SMEM((MICRO, 3), jnp.int32),
        pltpu.VMEM((MICRO, ROWS, WIDTH), BF16),
        pltpu.VMEM((MICRO, ROWS, WIDTH), BF16),
        pltpu.VMEM((HEADS, HEAD, HEAD), BF16),
        pltpu.VMEM((HEADS, HEAD, HEAD), BF16),
        wide,
        pltpu.VMEM((HEADS, tokens, HEAD), BF16),
        wide, wide, wide, wide, wide, wide,
        wide, wide, wide,
        pltpu.VMEM((HEADS, tokens, 2 * HEAD), BF16),
        pltpu.VMEM((MICRO, ROWS, HEAD), F32),
        pltpu.VMEM((MICRO, ROWS, HEAD), F32),
        tiles(),
        pltpu.VMEM((MICRO, ROWS, HEAD), F32),
        seg, seg, seg, seg, seg,
        tiles(MICRO, 2), tiles(MICRO), tiles(NZ - 1, MICRO),
        tiles(MICRO, 2, dtype=BF16), tiles(NZ - 1, MICRO, 2, dtype=BF16),
        tiles(MICRO, 2, dtype=BF16), tiles(NX - 1, MICRO, 2, dtype=BF16),
        tiles(MICRO, dtype=BF16), tiles(NZ - 1, MICRO, dtype=BF16),
        tiles(MICRO, dtype=BF16), tiles(NX - 1, MICRO, dtype=BF16),
        tiles(MICRO), tiles(MICRO), tiles(MICRO, 2), tiles(MICRO),
        tiles(), tiles(NY - 1),
        pltpu.VMEM((MICRO, ROWS, 128), F32),
        tiles(GROUPS), tiles(GROUPS, NY - 1),
        pltpu.VMEM((3, HEADS, 8, HEAD), F32),
        tiles(3), tiles(NZ - 1, 3), tiles(3), tiles(NX - 1, 3),
        pltpu.VMEM((HEADS, HEAD, tokens), BF16),
        pltpu.VMEM((HEADS, NX, NZ, 16, HEAD), BF16),
        pltpu.VMEM((HEADS, NX - 1, NZ, 16, HEAD), BF16),
        pltpu.VMEM((HEADS, NZ, 16, HEAD), BF16),
        pltpu.VMEM((HEADS, NZ - 1, 16, HEAD), BF16),
        pltpu.VMEM((NZ - 1, NX, 16, HEAD), BF16),
        pltpu.VMEM((NX, 16, HEAD), BF16),
        pltpu.VMEM((NX - 1, 16, HEAD), BF16),
        dma((9,)),
    ]
    scratch += [dma((NY - 1,))] * 2 + [dma((GROUPS, NY - 1))] * 2
    scratch += ([dma((GROUPS, NZ - 1))] * 2 + [dma((GROUPS, NX - 1))] * 2) * 2
    scratch += [dma((MICRO,))] * 2
    scratch += [dma((NZ - 1,))] * 2 + [dma((NX - 1,))] * 2
    scratch += [dma((HEADS, NX - 1))] * 2 + [dma((HEADS, NZ - 1))] * 2 + [dma((2, NZ - 1))] * 2
    scratch += [dma((2, NX - 1, NZ))] * 2 + [pltpu.SemaphoreType.REGULAR]
    scratch += [dma((NZ - 1,))] * 2 + [dma((NX - 1,))] * 4 + [dma((NZ - 1,))] * 2

    hbm = pl.BlockSpec(memory_space=pltpu.HBM)
    vmem = pl.BlockSpec(memory_space=pltpu.VMEM)
    input_grads, weight_sums, vector_sums = pl.pallas_call(
        body,
        out_shape=(
            jax.ShapeDtypeStruct((MICRO, ROWS, WIDTH), BF16),
            jax.ShapeDtypeStruct((NX, NZ, HEADS, 16, HEAD), BF16),
            jax.ShapeDtypeStruct((3, 8, 128), F32),
        ),
        in_specs=[hbm] * 9,
        out_specs=(vmem, vmem, vmem),
        scratch_shapes=scratch,
        compiler_params=pltpu.CompilerParams(
            collective_id=0, has_side_effects=True, vmem_limit_bytes=48 << 20
        ),
        name="rglru_backward",
    )(*(pltpu.with_memory_space_constraint(v, pltpu.HBM) for v in arguments))
    square = jax.ShapeDtypeStruct((1, HEADS, HEAD, HEAD), F32)
    input_grads, rate_grad, input_grad, vector_grads = pl.pallas_call(
        hand_out,
        out_shape=(
            jax.ShapeDtypeStruct((1, MICRO, ROWS, WIDTH), BF16), square, square,
            jax.ShapeDtypeStruct((3, 8, 128), F32),
        ),
        in_specs=[vmem] * 3,
        out_specs=(hbm, hbm, hbm, hbm),
        scratch_shapes=[
            pltpu.VMEM((2, HEADS, HEAD, HEAD), F32), pltpu.VMEM((3, 8, 128), F32), dma((2 + 2 * HEADS,)),
        ],
        compiler_params=pltpu.CompilerParams(vmem_limit_bytes=8 << 20),
        name="hand_out",
    )(input_grads, weight_sums, vector_sums)
    return (input_grads, rate_grad, input_grad, vector_grads.reshape(1, 3, WIDTH))


def solution(mesh):
    in_specs = (
        P("section", None, "seq", "chan"),
        P(None, "seq", "chan"),
        P("section", "chan", None, None),
        P("section", "chan", None, None),
        P("section", "chan"),
        P("section", "chan"),
        P("section", "chan"),
        P("section", "chan"),
        P(),
    )
    out_specs = (
        P("section", None, "seq", "chan"),
        P("section", "chan", None, None),
        P("section", "chan", None, None),
        P("section", None, "chan"),
    )
    return jax.shard_map(
        on_device, mesh=mesh, in_specs=in_specs, out_specs=out_specs, check_vma=False
    )
```
